32 devices in a mesh: dp: 4 (over y, x), ctx: 2 (over core), tensor: 4 (over z).
Axes of the slice: x: 2, y: 2, z: 4, core: 2. Of those that a mesh axis runs over, the one named last changes fastest.
Arguments:
- hidden: bfloat16 [16, 512, 768], P('dp', 'ctx'), may hold values from -6 to 6
- query: bfloat16 [16, 512, 768], P('dp', 'ctx'), may hold values from -6 to 6
- memory: bfloat16 [16, 384, 768], P('dp', 'ctx'), may hold values from -6 to 6
- cot_hidden: bfloat16 [16, 512, 768], P('dp', 'ctx'), may hold values from -6 to 6
- cot_query: bfloat16 [16, 512, 768], P('dp', 'ctx'), may hold values from -6 to 6
- lengths: int32 [16], P('dp'), may hold values from 64 to 512, as said below
- ranks: int32 [16, 512], P('dp'), may hold values from 0 to 511, each once within a row
- segments: int32 [16, 896], P('dp'), may hold values from 0 to 3, never falling along the last dimension, each value on 1 to 448 neighbouring positions
- w_query: bfloat16 [768, 768], P(None, 'tensor'), may hold values from -0.21875 to 0.21875
- w_key: bfloat16 [768, 768], P(None, 'tensor'), may hold values from -0.21875 to 0.21875
- w_value: bfloat16 [768, 768], P(None, 'tensor'), may hold values from -0.21875 to 0.21875
- w_rel: bfloat16 [768, 768], P(None, 'tensor'), may hold values from -0.21875 to 0.21875
- w_out: bfloat16 [768, 768], P('tensor'), may hold values from -4 to 4
- bias_word: float32 [12, 64], P('tensor'), may hold values from -3 to 3
- bias_rel: float32 [12, 64], P('tensor'), may hold values from -3 to 3
- bias_seg: float32 [12, 64], P('tensor'), may hold values from -3 to 3
- seg_embed: float32 [2, 12, 64], P(None, 'tensor'), may hold values from -0.75 to 0.75
- norm1_gain: float32 [768], replicated, may hold values from 0.5 to 1.5
- norm1_bias: float32 [768], replicated, may hold values from -1 to 1
- w_inner: bfloat16 [768, 3072], P(None, 'tensor'), may hold values from -0.21875 to 0.21875
- b_inner: float32 [3072], P('tensor'), may hold values from -1 to 1
- w_outer: bfloat16 [3072, 768], P('tensor'), may hold values from -0.109375 to 0.109375
- b_outer: float32 [768], replicated, may hold values from -1 to 1
- norm2_gain: float32 [768], replicated, may hold values from 0.5 to 1.5
- norm2_bias: float32 [768], replicated, may hold values from -1 to 1
Outputs:
- out_hidden: float32 [16, 512, 768], P('dp', ('ctx', 'tensor'))
- out_query: float32 [16, 512, 768], P('dp', ('ctx', 'tensor'))
- grad_hidden: float32 [16, 512, 768], P('dp', ('ctx', 'tensor'))
- grad_query: float32 [16, 512, 768], P('dp', ('ctx', 'tensor'))
- grad_w_query: float32 [768, 768], P(None, 'tensor')
- grad_w_key: float32 [768, 768], P(None, 'tensor')
- grad_w_value: float32 [768, 768], P(None, 'tensor')
- grad_w_rel: float32 [768, 768], P(None, 'tensor')
- grad_w_out: float32 [768, 768], P('tensor')
- grad_bias_word: float32 [12, 64], P('tensor')
- grad_bias_rel: float32 [12, 64], P('tensor')
- grad_bias_seg: float32 [12, 64], P('tensor')
- grad_seg_embed: float32 [2, 12, 64], P(None, 'tensor')
- grad_norm1_gain: float32 [768], P('tensor')
- grad_norm1_bias: float32 [768], P('tensor')
- grad_w_inner: float32 [768, 3072], P(None, 'tensor')
- grad_b_inner: float32 [3072], P('tensor')
- grad_w_outer: float32 [3072, 768], P('tensor')
- grad_b_outer: float32 [768], P('tensor')
- grad_norm2_gain: float32 [768], P('tensor')
- grad_norm2_bias: float32 [768], P('tensor')
The draws below stay inside these ranges and needn't reach their ends.
Inputs may be any that keep to these rules, and one draw needn't show every extreme that they name: `lengths`: in each aligned block of 4 sequences one has exactly 512 rows. `ranks`: each row is a permutation of the positions. `segments`: segment ids never fall along a row.
All inputs are finite; a program needn't handle non-finite values.
Results may differ from the reference program's by a relative error of at most 0.025.
Values may be sent and summed in bfloat16 or wider, within the bound.
No kernel may reach another device: no remote copies, remote signals or barrier semaphores. Data moves between devices by JAX's collectives and lax.ppermute only.
A program may use at most 256 MiB of HBM per device.

```python
import math
import jax
import jax.numpy as jnp
import numpy as np
from jax import lax

D = 768
NH = 12
DH = 64
FF = 3072
L = 512
M = 384
LEN_MIN = 64
SEQ_DEV = 4
SEQS = 16


def draw_lengths(key, part):
    base_len = jax.random.randint(jax.random.fold_in(key, 11), (SEQS,), LEN_MIN, L + 1)
    chosen = jax.random.randint(jax.random.fold_in(key, 12), (SEQS // SEQ_DEV,), 0, SEQ_DEV)
    index_all = jnp.arange(SEQS)
    full_one = index_all % SEQ_DEV == chosen[index_all // SEQ_DEV]
    return jnp.where(full_one, L, base_len).astype(jnp.int32)


def levels(rng, shape, shards, least, top_value):
    def one(dim, shards_of):
        steps = jax.random.uniform(jax.random.fold_in(jax.random.fold_in(rng, 6), dim), (shards_of,), jnp.float32, least / len(shards), top_value / len(shards))
        return jnp.repeat(jnp.exp(steps), shape[dim] // shards_of).reshape((-1,) + (1,) * (len(shape) - dim - 1))

    factor_of = one(*shards[0])
    for cut in shards[1:]:
        factor_of = factor_of * one(*cut)
    return factor_of


def split_up(amount, total, limit, slope):
    loads = [(1 << 20) // math.isqrt(grade ** slope) + 1 for grade in range(2, amount + 1)]
    rest, holding = total - limit - (amount - 1), [1] * (amount - 1)
    while rest > 0:
        free = [i for i in range(amount - 1) if holding[i] < limit]
        whole, remaining = sum([loads[i] for i in free]), rest
        for i in free:
            more = min(limit - holding[i], max(1, remaining * loads[i] // whole), rest)
            holding[i] = holding[i] + more
            rest = rest - more
    return np.array([limit] + holding)


def uneven(stream_key, amount, total, bound, skew):
    if amount == 2:
        one = jax.random.randint(stream_key, (), max(1, total - bound), min(bound, total - 1) + 1)
        return jnp.stack([one, total - one])
    tallies = jnp.asarray(split_up(amount, total, bound, skew), jnp.int32)
    couples = (amount - 1) // 2
    donor, taker = tallies[1:1 + 2 * couples:2], tallies[2:2 + 2 * couples:2]
    room = jnp.minimum(donor - 1, bound - taker)
    moved = jax.random.randint(jax.random.fold_in(stream_key, 1), (couples,), 0, 1 << 20) % (room + 1)
    tallies = tallies.at[1:1 + 2 * couples:2].set(donor - moved).at[2:2 + 2 * couples:2].set(taker + moved)
    return tallies[jax.random.permutation(jax.random.fold_in(stream_key, 2), amount)]


def centred(stream_key, shape, width, limit, pieces=(), kind=jnp.bfloat16):
    drawn = jax.random.normal(stream_key, shape, jnp.float32) * width
    if len(pieces) > 0:
        drawn = levels(stream_key, shape, pieces, -0.22, 0.18) * drawn
    return jnp.clip(drawn, min=-limit, max=limit).astype(kind)


def setup_inputs(seed: int = 0) -> dict:
    keys = jax.random.split(jax.random.key(seed), 26)
    hidden = centred(keys[0], (SEQS, L, D), 1.0, 6.0, ((0, 4), (1, 2)))
    query = centred(keys[1], (SEQS, L, D), 1.0, 6.0, ((0, 4), (1, 2)))
    memory = centred(keys[2], (SEQS, M, D), 1.0, 6.0, ((0, 4), (1, 2)))
    cot_hidden = centred(keys[3], (SEQS, L, D), 1.0, 6.0, ((0, 4), (1, 2)))
    cot_query = centred(keys[4], (SEQS, L, D), 1.0, 6.0, ((0, 4), (1, 2)))
    lengths = draw_lengths(jax.random.fold_in(keys[25], 71), 0)
    ranks = jax.vmap(lambda own: jax.random.permutation(own, L))(jax.random.split(keys[6], SEQS)).reshape((SEQS, L)).astype(jnp.int32)
    segments = jax.vmap(lambda own: jnp.searchsorted(jnp.cumsum(uneven(own, 4, M + L, (M + L) // 2, 0)), jnp.arange(M + L), side="right"))(jax.random.split(keys[7], SEQS)).reshape((SEQS, M + L)).astype(jnp.int32)
    w_query = centred(keys[8], (D, NH * DH), D ** -0.5, 0.21875, ((1, 4),))
    w_key = centred(keys[9], (D, NH * DH), D ** -0.5, 0.21875, ((1, 4),))
    w_value = centred(keys[10], (D, NH * DH), D ** -0.5, 0.21875, ((1, 4),))
    w_rel = centred(keys[11], (D, NH * DH), D ** -0.5, 0.21875, ((1, 4),))
    w_out = centred(keys[12], (NH * DH, D), 2 ** -0.5, 4.0, ((0, 4),))
    bias_word = centred(keys[13], (NH, DH), 0.5, 3.0, ((0, 4),), jnp.float32)
    bias_rel = centred(keys[14], (NH, DH), 0.5, 3.0, ((0, 4),), jnp.float32)
    bias_seg = centred(keys[15], (NH, DH), 0.5, 3.0, ((0, 4),), jnp.float32)
    seg_embed = centred(keys[16], (2, NH, DH), DH ** -0.5, 0.75, ((1, 4),), jnp.float32)
    norm1_gain = jnp.clip(1.0 + 0.1 * jax.random.normal(keys[17], (D,), jnp.float32), 0.5, 1.5)
    norm1_bias = centred(keys[18], (D,), 0.2, 1.0, (), jnp.float32)
    w_inner = centred(keys[19], (D, FF), D ** -0.5, 0.21875, ((1, 4),))
    b_inner = centred(keys[20], (FF,), 0.2, 1.0, ((0, 4),), jnp.float32)
    w_outer = centred(keys[21], (FF, D), FF ** -0.5, 0.109375, ((0, 4),))
    b_outer = centred(keys[22], (D,), 0.2, 1.0, (), jnp.float32)
    norm2_gain = jnp.clip(1.0 + 0.1 * jax.random.normal(keys[23], (D,), jnp.float32), 0.5, 1.5)
    norm2_bias = centred(keys[24], (D,), 0.2, 1.0, (), jnp.float32)
    return {"hidden": hidden, "query": query, "memory": memory, "cot_hidden": cot_hidden, "cot_query": cot_query, "lengths": lengths, "ranks": ranks, "segments": segments, "w_query": w_query, "w_key": w_key, "w_value": w_value, "w_rel": w_rel, "w_out": w_out, "bias_word": bias_word, "bias_rel": bias_rel, "bias_seg": bias_seg, "seg_embed": seg_embed, "norm1_gain": norm1_gain, "norm1_bias": norm1_bias, "w_inner": w_inner, "b_inner": b_inner, "w_outer": w_outer, "b_outer": b_outer, "norm2_gain": norm2_gain, "norm2_bias": norm2_bias}


precise = lax.Precision.HIGHEST
eps_norm = 1e-12

@jax.custom_vjp
def low(v):
    return lax.optimization_barrier(v.astype(jnp.bfloat16)).astype(jnp.float32)

@jax.custom_vjp
def low_back(v):
    return v

def low_keep(v):
    return (low(v), None)

def low_pass(kept, grad):
    return (grad,)

def back_keep(v):
    return (v, None)

def back_low(kept, grad):
    return (low(grad),)
low.defvjp(low_keep, low_pass)
low_back.defvjp(back_keep, back_low)

def sinusoid_table():
    positions = jnp.arange(M + L, -L, -1).astype(jnp.float32)
    frequency = 1.0 / 10000.0 ** (jnp.arange(0, D, 2).astype(jnp.float32) / D)
    angles = positions[:, None] * frequency[None, :]
    return jnp.concatenate([jnp.sin(angles), jnp.cos(angles)], 1)

def shift_rows(full_rows, offset, key_count):
    leading = full_rows.shape[:-2]
    row_count = full_rows.shape[-2]
    col_count = full_rows.shape[-1]
    flattened = full_rows.reshape(leading + (row_count * col_count,))
    kept_part = lax.slice_in_dim(flattened, offset, offset + row_count * (col_count - 1), axis=flattened.ndim - 1)
    return kept_part.reshape(leading + (row_count, col_count - 1))[..., :key_count]

def gelu_tanh(pre_value):
    return 0.5 * pre_value * (1.0 + jnp.tanh(0.7978845608028654 * (pre_value + 0.044715 * pre_value ** 3)))

def layer_norm(residual, gain_vec, bias_vec):
    centered = residual - lax.optimization_barrier(jnp.mean(residual, -1, keepdims=True))
    inv_std = lax.rsqrt(lax.optimization_barrier(jnp.mean(centered * centered, -1, keepdims=True)) + eps_norm)
    return centered * inv_std * gain_vec + bias_vec

def project(rows_in, weight):
    return jnp.einsum('btd,de->bte', rows_in, weight, precision=precise)

def layer_forward(params, hidden, query, memory, lengths, ranks, segments):
    w_query, w_key, w_value, w_rel, w_out, bias_word, bias_rel, bias_seg, seg_embed, norm1_gain, norm1_bias, w_inner, b_inner, w_outer, b_outer, norm2_gain, norm2_bias = params
    batch_size = hidden.shape[0]
    key_in = jnp.concatenate([memory, hidden], 1)
    key_rows = low(low_back(project(key_in, w_key))).reshape(batch_size, M + L, NH, DH)
    value_rows = low(low_back(project(key_in, w_value))).reshape(batch_size, M + L, NH, DH)
    pos_table = low(sinusoid_table())
    table_rows = jnp.broadcast_to(pos_table, (batch_size,) + pos_table.shape)
    rel_keys = low(low_back(project(table_rows, w_rel))).reshape(batch_size, M + 2 * L, NH, DH)
    key_valid = jnp.arange(L)[None, :] < lengths[:, None]
    mem_ok = jnp.ones((batch_size, L, M), dtype=bool)
    content_ok = jnp.concatenate([mem_ok, key_valid[:, None, :] & (ranks[:, None, :] <= ranks[:, :, None])], 2)
    query_ok = jnp.concatenate([mem_ok, key_valid[:, None, :] & (ranks[:, None, :] < ranks[:, :, None])], 2)
    differ = (segments[:, M:][:, :, None] != segments[:, None, :]).astype(jnp.float32)
    score_scale = 1.0 / math.sqrt(DH)

    def attend(stream, allowed):
        q_raw = low_back(project(stream, w_query)).reshape(batch_size, L, NH, DH)
        q_word = low(q_raw + bias_word)
        q_rel = low(q_raw + bias_rel)
        q_seg = q_raw + bias_seg
        content = jnp.einsum('bind,bjnd->bnij', q_word, key_rows, precision=precise)
        position = shift_rows(jnp.einsum('bind,bpnd->bnip', q_rel, rel_keys, precision=precise), L, M + L)
        seg_side = jnp.einsum('bind,knd->bnik', q_seg, seg_embed, precision=precise)
        segment_term = seg_side[..., 0:1] + differ[:, None] * (seg_side[..., 1:2] - seg_side[..., 0:1])
        raw_scores = low_back(content + position + segment_term)
        scores = jnp.where(allowed[:, None], raw_scores * score_scale, -1e+30)
        probabilities = jax.nn.softmax(scores, axis=-1)
        attended = low(low_back(jnp.einsum('bnij,bjnd->bind', low(probabilities), value_rows, precision=precise)))
        return low_back(project(attended.reshape(batch_size, L, NH * DH), w_out))

    def finish(stream, attn_out):
        normed1 = layer_norm(stream + attn_out, norm1_gain, norm1_bias)
        pre_act = low_back(project(low(normed1), w_inner)) + b_inner
        acted = low(gelu_tanh(pre_act))
        outer_out = low_back(project(acted, w_outer)) + b_outer
        return layer_norm(normed1 + outer_out, norm2_gain, norm2_bias)
    return (finish(hidden, attend(hidden, content_ok)), finish(query, attend(query, query_ok)))

def reference(hidden, query, memory, cot_hidden, cot_query, lengths, ranks, segments, w_query, w_key, w_value, w_rel, w_out, bias_word, bias_rel, bias_seg, seg_embed, norm1_gain, norm1_bias, w_inner, b_inner, w_outer, b_outer, norm2_gain, norm2_bias):
    params = tuple((weight.astype(jnp.float32) for weight in (w_query, w_key, w_value, w_rel, w_out, bias_word, bias_rel, bias_seg, seg_embed, norm1_gain, norm1_bias, w_inner, b_inner, w_outer, b_outer, norm2_gain, norm2_bias)))

    def pair_step(totals, entry):
        h_pair, q_pair, m_pair, ch_pair, cq_pair, len_pair, rank_pair, seg_pair = entry

        def forward(weights, h_in, q_in):
            return layer_forward(weights, h_in, q_in, m_pair, len_pair, rank_pair, seg_pair)
        results, pullback = jax.vjp(forward, params, h_pair, q_pair)
        param_grads, grad_h, grad_q = pullback((ch_pair, cq_pair))
        totals = jax.tree.map(jnp.add, totals, param_grads)
        return (totals, (results[0], results[1], grad_h, grad_q))
    groups = SEQS // 2
    floats = tuple((array_in.astype(jnp.float32) for array_in in (hidden, query, memory, cot_hidden, cot_query)))
    stacked = tuple((array_in.reshape((groups, 2) + array_in.shape[1:]) for array_in in floats + (lengths, ranks, segments)))
    zero_grads = tuple((jnp.zeros_like(weight) for weight in params))
    totals, (out_h, out_q, grad_h, grad_q) = lax.scan(pair_step, zero_grads, stacked)
    full_shape = (SEQS, L, D)
    return (out_h.reshape(full_shape), out_q.reshape(full_shape), grad_h.reshape(full_shape), grad_q.reshape(full_shape), totals[0], totals[1], totals[2], totals[3], totals[4], totals[5], totals[6], totals[7], totals[8], totals[9], totals[10], totals[11], totals[12], totals[13], totals[14], totals[15], totals[16])
```

```python
from functools import partial
import math

import jax
import jax.numpy as jnp
from jax import lax
from jax.experimental import pallas as pl
from jax.experimental.pallas import tpu as pltpu
from jax.sharding import PartitionSpec as P

D = 768
DH = 64
L = 512
M = 384
KT = M + L
RQ = 256
WIN = RQ + KT
HB = 128
WB = KT + HB
LANES = 128
NEG = -1e30
EPS = 1e-12
bf16 = jnp.bfloat16
f32 = jnp.float32


def dot(a, b):
    return lax.dot_general(a, b, (((1,), (0,)), ((), ())), preferred_element_type=f32)


def dot_nt(a, b):
    return lax.dot_general(a, b, (((1,), (1,)), ((), ())), preferred_element_type=f32)


def dot_tn(a, b):
    return lax.dot_general(a, b, (((0,), (0,)), ((), ())), preferred_element_type=f32)


def iota(shape, dim):
    return lax.broadcasted_iota(jnp.int32, shape, dim)


def row_to_col(row, n):
    return jnp.transpose(jnp.broadcast_to(row, (LANES, n)))


def pad_rows(dst, src, count):
    dst[:count, :] = src
    dst[count:, :] = jnp.zeros((dst.shape[0] - count, dst.shape[1]), dst.dtype)


def seg_parts(qs, se_ref, seg_col, scale):
    d_i = iota((2 * LANES, LANES), 0)
    l_i = iota((2 * LANES, LANES), 1)
    head_of_lane = jnp.where(l_i < 8, 0, jnp.where(l_i < 16, 1, jnp.where((l_i >= 64) & (l_i < 72), 2, -1)))
    pick = ((d_i // DH) == head_of_lane).astype(bf16)
    sides = []
    for s in range(2):
        prod = qs * se_ref[s : s + 1, :] * scale
        hi = prod.astype(bf16)
        lo = (prod - hi.astype(f32)).astype(bf16)
        sides.append(dot(hi, pick) + dot(lo, pick))
    lane = iota(sides[0].shape, 1)
    val = jnp.where((lane & 3) == seg_col, sides[0], sides[1])
    hi = val.astype(bf16).astype(f32)
    lo = val - hi
    return jnp.where((lane & 7) < 4, hi, lo)


def head_mask(h, shape):
    return (iota(shape, 1) // DH) == (h & 1)


def ext_mask(h, shape):
    return (iota(shape, 1) // 8) == (h if h < 2 else 8)


def attn_fwd_kernel(
    meta, hid, qry, mem, hid_o, mem_o, ranks, segs, wq, wk, wv, rk, bw, br, bs, se,
    att_out, p_out, kx_out, v_out, wq_s, wk_s, wv_s, key_s, ma_s, word_s, rel_s, ext_s,
):
    step = pl.program_id(0)
    s = step + meta[meta.shape[0] - 1]
    c = meta[0]
    length = meta[1 + s]

    @pl.when(step == 0)
    def _():
        pad_rows(wq_s, wq[...], 3 * DH)
        pad_rows(wk_s, wk[...], 3 * DH)
        pad_rows(wv_s, wv[...], 3 * DH)

    rm = mem.shape[1]
    rh = hid.shape[1]
    key_s[pl.ds(pl.multiple_of(c * rm, 64), rm), :] = mem[0]
    key_s[pl.ds(pl.multiple_of((1 - c) * rm, 64), rm), :] = mem_o[0]
    key_s[pl.ds(pl.multiple_of(M + c * rh, 64), rh), :] = hid[0]
    key_s[pl.ds(pl.multiple_of(M + (1 - c) * rh, 64), rh), :] = hid_o[0]

    seg_row = segs[pl.ds(s, 1), :]
    own_seg = jnp.where(c == 0, seg_row[:, M : M + RQ], seg_row[:, M + RQ :])
    seg_col = row_to_col(own_seg.astype(f32), RQ).astype(jnp.int32)
    rank_row = ranks[pl.ds(s, 1), :]
    own_rank = jnp.where(c == 0, rank_row[:, :RQ], rank_row[:, RQ:])
    thr_col = row_to_col(own_rank.astype(f32), RQ)[:, :1]
    valid = iota((1, L), 1) < length
    key_rank = jnp.where(valid, rank_row, 1 << 20).astype(f32)
    ma_s[0] = jnp.where(key_rank <= thr_col, 0.0, NEG)
    ma_s[1] = jnp.where(key_rank < thr_col, 0.0, NEG)

    hot = ((iota((LANES, KT), 0) & 3) == seg_row).astype(f32)
    hot = jnp.transpose(hot)
    keys = dot_nt(key_s[...], wk_s[...])
    kx_out[0, :, :LANES] = keys[:, :LANES].astype(bf16)
    kx_out[0, :, LANES : 2 * LANES] = hot.astype(bf16)
    k2 = jnp.where(iota((KT, LANES), 1) < DH, keys[:, LANES:], hot)
    kx_out[0, :, 2 * LANES :] = k2.astype(bf16)
    v_out[0] = dot_nt(key_s[...], wv_s[...]).astype(bf16)

    scale = 1.0 / math.sqrt(DH)
    for a, x_ref in enumerate((hid, qry)):
        q_raw = dot_nt(x_ref[0], wq_s[...])
        word_s[a] = ((q_raw + bw[...]) * scale).astype(bf16)
        rel_s[a] = ((q_raw + br[...]) * scale).astype(bf16)
        ext_s[a] = seg_parts(q_raw + bs[...], se, seg_col, scale).astype(bf16)

    zero_b = jnp.zeros((), bf16)
    nt = att_out.shape[0]
    rr = RQ // nt

    def stream(a, carry):
        outs = []
        for h in range(3):
            lo = (h // 2) * LANES
            w_h = word_s[a, :, lo : lo + LANES]
            e_h = jnp.where(ext_mask(h, (RQ, LANES)), ext_s[a], zero_b)
            if h < 2:
                qx = jnp.concatenate([jnp.where(head_mask(h, w_h.shape), w_h, zero_b), e_h], 1)
                kx = kx_out[0, :, : 2 * LANES]
            else:
                qx = jnp.where(head_mask(h, w_h.shape), w_h, e_h)
                kx = kx_out[0, :, 2 * LANES :]
            r_h = rel_s[a, :, lo : lo + LANES]
            qr = jnp.where(head_mask(h, r_h.shape), r_h, zero_b)
            content = dot_nt(qx, kx)
            for i0 in (0, HB):
                w0 = HB - i0
                pos = dot_nt(qr[i0 : i0 + HB], rk[w0 : w0 + WB, lo : lo + LANES])
                pos = pltpu.roll(pos, WB - HB, 1, stride=1, stride_axis=0)[:, :KT]
                sc = content[i0 : i0 + HB] + pos
                sc = jnp.concatenate([sc[:, :M], sc[:, M:] + ma_s[a, i0 : i0 + HB, :]], 1)
                top = jnp.max(sc, -1, keepdims=True)
                e = jnp.exp(sc - top)
                inv = 1.0 / jnp.sum(e, -1, keepdims=True)
                p_out[0, h, a, i0 : i0 + HB, :] = (e * inv).astype(bf16)
            outs.append(dot(p_out[0, h, a], v_out[0, :, lo : lo + LANES]))
        o01 = jnp.where(head_mask(0, outs[0].shape), outs[0], outs[1]).astype(bf16)
        o2 = outs[2][:, :DH].astype(bf16)
        for t in range(nt):
            att_out[t, a, 0, :, :LANES] = o01[t * rr : (t + 1) * rr]
            att_out[t, a, 0, :, LANES:] = o2[t * rr : (t + 1) * rr]
        return carry

    lax.fori_loop(0, 2, stream, 0)


def whole(shape):
    zeros = (0,) * len(shape)
    return pl.BlockSpec(shape, lambda s, *_: zeros)


def per_seq(shape, axis=0):
    return pl.BlockSpec(shape, lambda s, *_: tuple(s if d == axis else 0 for d in range(len(shape))))


def from_seq(shape):
    return pl.BlockSpec(shape, lambda s, meta: (s + meta[meta.shape[0] - 1],) + (0,) * (len(shape) - 1))


def attn_fwd(meta, hid, qry, mem, hid_o, mem_o, ranks, segs, wq, wk, wv, rk, bw, br, bs, se, n_t, count):
    _, rh, _ = hid.shape
    rm = mem.shape[1]
    hc = wq.shape[0]
    rr = rh // n_t
    seq = from_seq
    grid_spec = pltpu.PrefetchScalarGridSpec(
        num_scalar_prefetch=1,
        grid=(count,),
        in_specs=[
            seq((1, rh, D)), seq((1, rh, D)), seq((1, rm, D)), seq((1, rh, D)), seq((1, rm, D)),
            whole(ranks.shape), whole(segs.shape), whole(wq.shape), whole(wk.shape), whole(wv.shape),
            whole(rk.shape), whole(bw.shape), whole(br.shape), whole(bs.shape), whole(se.shape),
        ],
        out_specs=[
            per_seq((n_t, 2, 1, rr, hc), 2), per_seq((1, 3, 2, rh, KT)), per_seq((1, KT, 3 * LANES)),
            per_seq((1, KT, 2 * LANES)),
        ],
        scratch_shapes=[
            pltpu.VMEM((2 * LANES, D), bf16), pltpu.VMEM((2 * LANES, D), bf16), pltpu.VMEM((2 * LANES, D), bf16),
            pltpu.VMEM((KT, D), bf16), pltpu.VMEM((2, RQ, L), f32), pltpu.VMEM((2, RQ, 2 * LANES), bf16),
            pltpu.VMEM((2, RQ, 2 * LANES), bf16), pltpu.VMEM((2, RQ, LANES), bf16),
        ],
    )
    return pl.pallas_call(
        attn_fwd_kernel,
        grid_spec=grid_spec,
        out_shape=[
            jax.ShapeDtypeStruct((n_t, 2, count, rr, hc), bf16),
            jax.ShapeDtypeStruct((count, 3, 2, rh, KT), bf16),
            jax.ShapeDtypeStruct((count, KT, 3 * LANES), bf16),
            jax.ShapeDtypeStruct((count, KT, 2 * LANES), bf16),
        ],
        compiler_params=pltpu.CompilerParams(vmem_limit_bytes=56 << 20),
        cost_estimate=pl.CostEstimate(flops=count * 10**10, bytes_accessed=count * 16 * 10**6, transcendentals=count * 10**6),
        name="attn_fwd",
    )(meta, hid, qry, mem, hid_o, mem_o, ranks, segs, wq, wk, wv, rk, bw, br, bs, se)


SUM_ROWS = 16


def attn_bwd_kernel(
    meta, p_in, datt, kx, v, hid, qry, mem, hid_o, mem_o, segs, wq, rk, table, bw, br, bs, se,
    dq_out, dkv_own, dkv_oth, gw_own, gw_oth,
    wq_s, key_s, do_s, x_s, word_s, rel_s, qs_s, ds_s, sk_s, dkv_s, dw_s, dr_s, dg_s, g_a, gr_a, sm_a,
):
    step = pl.program_id(0)
    s = step + meta[meta.shape[0] - 1]
    c = meta[0]
    rm = mem.shape[1]
    rh = hid.shape[1]
    hc = 3 * DH

    @pl.when(step == 0)
    def _():
        pad_rows(wq_s, wq[...], hc)
        do_s[:, :, hc:] = jnp.zeros((2, RQ, do_s.shape[2] - hc), bf16)
        for acc in (g_a, gr_a, sm_a):
            acc[...] = jnp.zeros(acc.shape, f32)

    key_s[pl.ds(pl.multiple_of(c * rm, 64), rm), :] = mem[0]
    key_s[pl.ds(pl.multiple_of((1 - c) * rm, 64), rm), :] = mem_o[0]
    key_s[pl.ds(pl.multiple_of(M + c * rh, 64), rh), :] = hid[0]
    key_s[pl.ds(pl.multiple_of(M + (1 - c) * rh, 64), rh), :] = hid_o[0]

    flip = (iota((RQ, RQ), 0) + iota((RQ, RQ), 1) == RQ - 1).astype(bf16)
    seg_row = segs[pl.ds(s, 1), :]
    own_seg = jnp.where(c == 0, seg_row[:, M : M + RQ], seg_row[:, M + RQ :])
    seg_col = dot(flip, row_to_col(own_seg.astype(f32), RQ).astype(bf16)).astype(jnp.int32)

    nt = datt.shape[0]
    rr = RQ // nt
    for a, x_ref in enumerate((hid, qry)):
        x_rev = dot(flip, x_ref[0]).astype(bf16)
        x_s[a] = x_rev
        q_raw = dot_nt(x_rev, wq_s[...])
        word_s[a] = (q_raw + bw[...]).astype(bf16)
        rel_s[a] = (q_raw + br[...]).astype(bf16)
        qs_s[a] = q_raw + bs[...]
        for t in range(nt):
            do_s[a, t * rr : (t + 1) * rr, :hc] = datt[t, a, 0]

    scale = 1.0 / math.sqrt(DH)
    zero_b = jnp.zeros((), bf16)
    dk_t, dv_t = [None, None], [None, None]
    lane = iota((RQ, LANES), 1)
    first_head = head_mask(0, (RQ, LANES))
    for h in range(3):
        pair = h // 2
        cols = slice(pair * LANES, (pair + 1) * LANES)
        mask2 = head_mask(h, (2 * RQ, LANES))
        kcols = slice(0, 2 * LANES) if h < 2 else slice(2 * LANES, 3 * LANES)
        base = 0 if h < 2 else 64
        own = lane - base == seg_col
        rest = (lane >= base) & (lane < base + 4) & (~own)

        def merge(dst, a, new):
            if h == 0:
                dst[a, :, cols] = new
            elif h == 1:
                dst[a, :, cols] = jnp.where(first_head, dst[a, :, cols], new)
            else:
                dst[a, :, cols] = jnp.where(first_head, new, 0.0)

        def stream(a):
            do_h = jnp.where(head_mask(h, (RQ, LANES)), do_s[a, :, cols], zero_b)
            do_r = (dot(flip, do_h) * scale).astype(bf16)
            pf = dot(flip, p_in[0, h, a])
            dp = dot_nt(do_r, v[0, :, cols])
            t = pf * dp
            delta = jnp.sum(t, -1, keepdims=True)
            ds = t - pf * delta
            ds_s[a] = ds.astype(bf16)
            for half, u0 in enumerate((0, HB)):
                blk = jnp.concatenate([ds[u0 : u0 + HB], jnp.zeros((HB, WB - KT), f32)], 1)
                sk_s[half, a] = pltpu.roll(blk, 1, 1, stride=1, stride_axis=0).astype(bf16)
            dqx = dot(ds_s[a], kx[0, :, kcols])
            side = dqx[:, LANES:] if h < 2 else dqx
            d0 = jnp.sum(jnp.where(own, side, 0.0), -1, keepdims=True)
            d1 = jnp.sum(jnp.where(rest, side, 0.0), -1, keepdims=True)
            merge(dw_s, a, dqx[:, :LANES])
            merge(dg_s, a, d0 * se[0:1, cols] + d1 * se[1:2, cols])
            qs = jnp.where(head_mask(h, (RQ, LANES)), qs_s[a, :, cols], 0.0)
            sm_a[3:4, cols] += jnp.sum(d0 * qs, 0, keepdims=True)
            sm_a[4:5, cols] += jnp.sum(d1 * qs, 0, keepdims=True)

        for a in range(2):
            stream(a)
        for half, u0 in enumerate((0, HB)):
            sk = sk_s[half].reshape(2 * HB, WB)
            dr = dot(sk, rk[u0 : u0 + WB, cols])
            for a in range(2):
                new = dr[a * HB : (a + 1) * HB]
                old = dr_s[a, u0 : u0 + HB, cols] if h == 1 else 0.0
                if h > 0:
                    hm = first_head[:HB]
                    new = jnp.where(hm, old, new) if h == 1 else jnp.where(hm, new, old)
                dr_s[a, u0 : u0 + HB, cols] = new
            r_h = jnp.concatenate([rel_s[a, u0 : u0 + HB, cols] for a in range(2)], 0)
            r_h = jnp.where(head_mask(h, r_h.shape), r_h, zero_b)
            gr_a[cols, u0 : u0 + WB] += dot_tn(r_h, sk)
        w_h = jnp.where(mask2, word_s[:, :, cols].reshape(2 * RQ, LANES), zero_b)
        part = dot_tn(w_h, ds_s[...].reshape(2 * RQ, KT))
        dk_t[pair] = part if dk_t[pair] is None else dk_t[pair] + part
        o_h = jnp.where(mask2, do_s[:, :, cols].reshape(2 * RQ, LANES), zero_b)
        part = dot_tn(o_h, p_in[0, h].reshape(2 * RQ, KT))
        dv_t[pair] = part if dv_t[pair] is None else dv_t[pair] + part

    for row, g in enumerate((dw_s, dr_s, dg_s)):
        sm_a[row : row + 1, :] += jnp.sum(g[0], 0, keepdims=True) + jnp.sum(g[1], 0, keepdims=True)
    for a in range(2):
        dq = (dw_s[a] + dr_s[a] + dg_s[a]).astype(bf16)
        g_a[0] += dot_tn(dq, x_s[a])
        dq_nat = dot(flip, dq).astype(bf16)
        for t in range(nt):
            dq_out[t, a, 0] = dq_nat[t * rr : (t + 1) * rr, :hc]

    for i, parts in enumerate((dk_t, dv_t)):
        g_t = jnp.concatenate(parts, 0)
        g_a[1 + i] += dot(g_t.astype(bf16), key_s[...])
        dkv_s[...] = jnp.transpose(g_t[:, M:])
        own_rows = dkv_s[pl.ds(pl.multiple_of(c * RQ, RQ), RQ), :hc].astype(bf16)
        oth_rows = dkv_s[pl.ds(pl.multiple_of((1 - c) * RQ, RQ), RQ), :hc].astype(bf16)
        for t in range(nt):
            dkv_own[t, i, 0] = own_rows[t * rr : (t + 1) * rr]
            dkv_oth[t, i, 0] = oth_rows[t * rr : (t + 1) * rr]

    @pl.when(step == pl.num_programs(0) - 1)
    def _():
        gr = dot(gr_a[...].astype(bf16), table[...])
        for i in range(2):
            rows = slice(i * hc, (i + 1) * hc)
            last = g_a[2, :hc] if i == 0 else gr[:hc]
            first = g_a[i, :hc]
            gw_own[rows, :] = jnp.where(c == 0, first, last).astype(bf16)
            gw_oth[rows, :] = jnp.where(c == 0, last, first).astype(bf16)
        hi = sm_a[...].astype(bf16)
        lo = (sm_a[...] - hi.astype(f32)).astype(bf16)
        sums = jnp.concatenate([hi, lo], 0)
        for dst in (gw_own, gw_oth):
            dst[2 * hc :, : 2 * LANES] = sums
            dst[2 * hc :, 2 * LANES :] = jnp.zeros((SUM_ROWS, D - 2 * LANES), bf16)


def attn_bwd(meta, p, datt, kx, v, hid, qry, mem, hid_o, mem_o, segs, wq, rk, table, bw, br, bs, se):
    _, rh, _ = hid.shape
    count = p.shape[0]
    rm = mem.shape[1]
    hc = wq.shape[0]
    n_t = datt.shape[0]
    rr = rh // n_t
    share = per_seq((n_t, 2, 1, rr, hc), 2)
    sds = jax.ShapeDtypeStruct
    rows_out = sds((n_t, 2, count, rr, hc), bf16)
    g_shape = (2 * hc + SUM_ROWS, D)
    grid_spec = pltpu.PrefetchScalarGridSpec(
        num_scalar_prefetch=1,
        grid=(count,),
        in_specs=[
            per_seq((1, 3, 2, rh, KT)), share, per_seq((1, KT, 3 * LANES)), per_seq((1, KT, 2 * LANES)),
            from_seq((1, rh, D)), from_seq((1, rh, D)), from_seq((1, rm, D)), from_seq((1, rh, D)), from_seq((1, rm, D)),
            whole(segs.shape), whole(wq.shape), whole(rk.shape), whole(table.shape),
            whole(bw.shape), whole(br.shape), whole(bs.shape), whole(se.shape),
        ],
        out_specs=[share, share, share, whole(g_shape), whole(g_shape)],
        scratch_shapes=[
            pltpu.VMEM((2 * LANES, D), bf16), pltpu.VMEM((KT, D), bf16), pltpu.VMEM((2, RQ, 2 * LANES), bf16),
            pltpu.VMEM((2, RQ, D), bf16), pltpu.VMEM((2, RQ, 2 * LANES), bf16), pltpu.VMEM((2, RQ, 2 * LANES), bf16),
            pltpu.VMEM((2, RQ, 2 * LANES), f32), pltpu.VMEM((2, RQ, KT), bf16), pltpu.VMEM((2, 2, HB, WB), bf16),
            pltpu.VMEM((L, 2 * LANES), f32), pltpu.VMEM((2, RQ, 2 * LANES), f32), pltpu.VMEM((2, RQ, 2 * LANES), f32),
            pltpu.VMEM((2, RQ, 2 * LANES), f32),
            pltpu.VMEM((3, 2 * LANES, D), f32), pltpu.VMEM((2 * LANES, WIN), f32), pltpu.VMEM((8, 2 * LANES), f32),
        ],
    )
    return pl.pallas_call(
        attn_bwd_kernel,
        grid_spec=grid_spec,
        out_shape=[rows_out, rows_out, rows_out, sds(g_shape, bf16), sds(g_shape, bf16)],
        compiler_params=pltpu.CompilerParams(vmem_limit_bytes=58 << 20),
        cost_estimate=pl.CostEstimate(flops=count * 10**10, bytes_accessed=count * 16 * 10**6, transcendentals=0),
        name="attn_bwd",
    )(meta, p, datt, kx, v, hid, qry, mem, hid_o, mem_o, segs, wq, rk, table, bw, br, bs, se)


def norm_bwd(d_out, scaled, inv_std, gain):
    e = d_out * gain
    return inv_std * (e - jnp.mean(e, -1, keepdims=True) - scaled * jnp.mean(e * scaled, -1, keepdims=True))


def norm_fwd(resid):
    cen = resid - jnp.mean(resid, -1, keepdims=True)
    inv_std = lax.rsqrt(jnp.mean(cen * cen, -1, keepdims=True) + EPS)
    return cen * inv_std, inv_std


GELU_A = 0.7978845608028654
GELU_B = 0.044715


def ffn_kernel(
    ti, att0, att1, hid, qry, cot_h, cot_q, wi_own, wo_own, wx_own, wgot, n1g, n1b, bo, n2g, n2b,
    out_h, out_q, dres_out, inner_out, act_out, dpre_out, dout_out, dattn_out, datt0, datt1, vec_out, gb_out,
    wi, wo, wx, n1_s, sc1_s, inv1_s, gp_s, acc_s, dres2_s, x_s, sems, sems_x,
):
    t_me = ti[0]
    n_t = att0.shape[0]
    hc = att0.shape[4]
    rows = dres_out.shape[0]
    half = rows // 2
    quarter = half // 2
    n_p = wgot.shape[0]
    parts = ((wx, wx_own), (wi, wi_own), (wo, wo_own))

    def piece_copy(i, k, j):
        dst = parts[i][0]
        count = dst.shape[1] // n_p
        start = ((wi.shape[1] + wo.shape[1]) // n_p, 0, wi.shape[1] // n_p)[i]
        return pltpu.make_async_copy(
            wgot.at[j, k - 1, pl.ds(start, count), :], dst.at[k, pl.ds(j * count, count), :], sems.at[i, k, j]
        )

    copies = []
    for i, (dst, own) in enumerate(parts):
        group = [[pltpu.make_async_copy(own, dst.at[0], sems.at[i, 0, 0])]]
        group += [[piece_copy(i, k, j) for j in range(n_p)] for k in range(1, n_t)]
        copies.append(group)
    rr = x_s.shape[2]
    mine = [
        pltpu.make_async_copy(x.at[:, pl.ds(t_me * rr, rr), :], x_s.at[i], sems_x.at[i])
        for i, x in enumerate((hid, qry, cot_h, cot_q))
    ]
    for copy in mine[:2]:
        copy.start()
    for per_k in copies[0]:
        for copy in per_k:
            copy.start()
    for copy in mine[2:]:
        copy.start()
    for k in range(n_t):
        for copy in copies[1][k] + copies[2][k]:
            copy.start()

    def wait(i):
        for per_k in copies[i]:
            for copy in per_k:
                copy.wait()

    halves = (slice(0, half), slice(half, rows))
    wait(0)
    for a in range(2):
        r = halves[a]
        mine[a].wait()
        acc = x_s[a].reshape(half, D).astype(f32)
        for k in range(n_t):
            z = t_me ^ k
            part = jnp.concatenate([att0[z, a].reshape(quarter, hc), att1[z, a].reshape(quarter, hc)], 0)
            acc = acc + dot(part, wx[k, :hc, :])
        scaled, inv_std = norm_fwd(acc)
        sc1_s[r, :] = scaled
        inv1_s[r, :] = jnp.broadcast_to(inv_std, (half, LANES))
        n1 = scaled * n1g[...] + n1b[...]
        n1_s[r, :] = n1
        inner_out[r, :] = n1.astype(bf16)
    acc_s[...] = jnp.zeros(acc_s.shape, f32)

    def up(k, carry):
        @pl.when(k == 0)
        def _():
            copies[1][0][0].wait()
            copies[2][0][0].wait()

        @pl.when(k > 0)
        def _():
            for i in (1, 2):
                for j in range(n_p):
                    piece_copy(i, k, j).wait()

        bias = wx[k, hc : hc + 1, :].astype(f32) + wx[k, hc + 1 : hc + 2, :].astype(f32)
        for r in halves:
            pre = dot(inner_out[r, :], wi[k]) + bias
            sq = pre * pre
            th = jnp.tanh(GELU_A * (pre + GELU_B * (pre * sq)))
            act_out[k, r, :] = (0.5 * pre * (1.0 + th)).astype(bf16)
            gp_s[k, r, :] = 0.5 * (1.0 + th) + (0.5 * pre) * (1.0 - th * th) * (GELU_A + (3.0 * GELU_A * GELU_B) * sq)
            acc_s[r, :] += dot(act_out[k, r, :], wo[k])
        return carry

    lax.fori_loop(0, n_t, up, 0)

    sums = [None] * 3
    for a, o_ref in enumerate((out_h, out_q)):
        r = halves[a]
        scaled, inv_std = norm_fwd(n1_s[r, :] + (acc_s[r, :] + bo[...]))
        o_ref[...] = scaled * n2g[...] + n2b[...]
        mine[2 + a].wait()
        cot = x_s[2 + a].reshape(half, D).astype(f32)
        d2 = norm_bwd(cot, scaled, inv_std, n2g[...])
        dres2_s[r, :] = d2
        dout_out[r, :] = d2.astype(bf16)
        for i, g in enumerate((cot * scaled, cot, d2)):
            g = jnp.sum(g, 0, keepdims=True)
            sums[i] = g if a == 0 else sums[i] + g
    vec_out[2:3, :] = sums[0]
    vec_out[3:4, :] = sums[1]
    vec_out[4:5, :] = sums[2]
    acc_s[...] = jnp.zeros(acc_s.shape, f32)

    def down(k, carry):
        total = None
        for r in halves:
            d_pre = dot_nt(dout_out[r, :], wo[k]) * gp_s[k, r, :]
            g = jnp.sum(d_pre, 0, keepdims=True)
            total = g if total is None else total + g
            dpre_out[k, r, :] = d_pre.astype(bf16)
            acc_s[r, :] += dot_nt(dpre_out[k, r, :], wi[k])
        gb_out[pl.ds(k, 1), :] = total
        return carry

    lax.fori_loop(0, n_t, down, 0)
    for a in range(2):
        r = halves[a]
        d_n1 = dres2_s[r, :] + acc_s[r, :]
        scaled = sc1_s[r, :]
        for i, g in enumerate((d_n1 * scaled, d_n1)):
            g = jnp.sum(g, 0, keepdims=True)
            vec_out[i : i + 1, :] = g if a == 0 else vec_out[i : i + 1, :] + g
        d1 = norm_bwd(d_n1, scaled, inv1_s[r, :1], n1g[...])
        dres_out[r, :] = d1
        dattn_out[r, :] = d1.astype(bf16)
        for k in range(n_t):
            z = t_me ^ k
            part = dot_nt(dattn_out[r, :], wx[k, :hc, :]).astype(bf16)
            datt0[z, a] = part[:quarter].reshape(datt0.shape[2:])
            datt1[z, a] = part[quarter:].reshape(datt1.shape[2:])


def ffn(ti, att0, att1, hid, qry, cot_h, cot_q, w_inner, w_outer, wx_own, wgot, n1g, n1b, bo, n2g, n2b):
    n_t, _, _, _, hc = att0.shape
    n_f = w_outer.shape[0]
    n_s, rr = hid.shape[0], hid.shape[1] // n_t
    half = n_s * rr
    rows = 2 * half
    sds = jax.ShapeDtypeStruct
    vm = pl.BlockSpec(memory_space=pltpu.VMEM)
    hbm = pl.BlockSpec(memory_space=pl.ANY)
    return pl.pallas_call(
        ffn_kernel,
        in_specs=[pl.BlockSpec(memory_space=pltpu.SMEM)] + [vm] * 2 + [hbm] * 8 + [vm] * 5,
        out_shape=[
            sds((half, D), f32), sds((half, D), f32), sds((rows, D), f32), sds((rows, D), bf16),
            sds((n_t, rows, n_f), bf16), sds((n_t, rows, n_f), bf16), sds((rows, D), bf16), sds((rows, D), bf16),
            sds(att0.shape, bf16), sds(att1.shape, bf16), sds((5, D), f32), sds((n_t, n_f), f32),
        ],
        scratch_shapes=[
            pltpu.VMEM((n_t,) + w_inner.shape, bf16), pltpu.VMEM((n_t,) + w_outer.shape, bf16),
            pltpu.VMEM((n_t,) + wx_own.shape, bf16),
            pltpu.VMEM((rows, D), f32), pltpu.VMEM((rows, D), f32), pltpu.VMEM((rows, LANES), f32),
            pltpu.VMEM((n_t, rows, n_f), f32), pltpu.VMEM((rows, D), f32), pltpu.VMEM((rows, D), f32),
            pltpu.VMEM((4, n_s, rr, D), bf16),
            pltpu.SemaphoreType.DMA((3, n_t, wgot.shape[0])), pltpu.SemaphoreType.DMA((4,)),
        ],
        compiler_params=pltpu.CompilerParams(vmem_limit_bytes=60 << 20),
        cost_estimate=pl.CostEstimate(flops=11 * 10**9, bytes_accessed=25 * 10**6, transcendentals=2 * 10**6),
        name="ffn",
    )(ti, att0, att1, hid, qry, cot_h, cot_q, w_inner, w_outer, wx_own, wgot, n1g, n1b, bo, n2g, n2b)


XROWS = 256


def wgrad_kernel(pos, inner, act, dpre, dout, att0, att1, dattn, vec, gb, ga_out, own_out, oth_out, gx_s):
    hc = att0.shape[4]
    n_p = ga_out.shape[0]
    d, c = pos[0], pos[1]
    k = pl.program_id(0)
    z = pos[2] ^ k
    n_i, n_o, n_x = D // n_p, act.shape[2] // n_p, XROWS // n_p
    rows = []
    for a in range(2):
        rows += [att0[z, a].reshape(-1, hc), att1[z, a].reshape(-1, hc)]
    gx_s[:hc, :] = dot_tn(jnp.concatenate(rows, 0), dattn[...])
    gx_s[hc:, :] = jnp.zeros((gx_s.shape[0] - hc, D), f32)
    gx_s[hc : hc + 1, :] = gb[pl.ds(k, 1), :]
    for t in range(D // hc):
        @pl.when(z == t)
        def _():
            gx_s[hc + 8 : hc + 13, :hc] = vec[:, t * hc : (t + 1) * hc]
    g = dot_tn(inner[...], dpre[0]).astype(bf16)
    x = gx_s[...].astype(bf16)
    for m in range(n_p // 2):
        halves = [jnp.concatenate([g[j * n_i : (j + 1) * n_i], x[j * n_x : (j + 1) * n_x]], 0) for j in (2 * m, 2 * m + 1)]
        own_out[m ^ d, 0] = jnp.where(c == 0, halves[0], halves[1])
        oth_out[m ^ d, 0] = jnp.where(c == 0, halves[1], halves[0])
    g = dot_tn(act[0], dout[...]).astype(bf16)
    for j in range(n_p):
        ga_out[j, 0] = g[j * n_o : (j + 1) * n_o]


def wgrad(pos, inner, act, dpre, dout, att0, att1, dattn, vec, gb, n_d):
    n_t, rows, n_f = act.shape
    n_p = 2 * n_d
    n_o = n_f // n_p
    rest = (D + XROWS) // n_p
    return pl.pallas_call(
        wgrad_kernel,
        grid=(n_t,),
        in_specs=[
            pl.BlockSpec(memory_space=pltpu.SMEM),
            whole(inner.shape), per_seq((1, rows, n_f)), per_seq((1, rows, n_f)), whole(dout.shape),
            whole(att0.shape), whole(att1.shape), whole(dattn.shape), whole(vec.shape), whole(gb.shape),
        ],
        out_specs=[per_seq((n_p, 1, n_o, D), 1)] + [per_seq((n_d, 1, rest, D), 1)] * 2,
        out_shape=[
            jax.ShapeDtypeStruct((n_p, n_t, n_o, D), bf16)
        ] + [jax.ShapeDtypeStruct((n_d, n_t, rest, D), bf16)] * 2,
        scratch_shapes=[pltpu.VMEM((XROWS, D), f32)],
        compiler_params=pltpu.CompilerParams(vmem_limit_bytes=60 << 20),
        cost_estimate=pl.CostEstimate(flops=6 * 10**9, bytes_accessed=20 * 10**6, transcendentals=0),
        name="wgrad",
    )(pos, inner, act, dpre, dout, att0, att1, dattn, vec, gb)


def final_kernel(ti, rows0, rows1, w_own, wgot, dres, gh, gq, w_s, sems):
    t_me = ti[0]
    n_t, _, n_s, rr, hc = rows0.shape
    n_p = wgot.shape[0]
    half = gh.shape[0]
    sub = half // 2
    count = wgot.shape[2]
    copies = [[pltpu.make_async_copy(w_own, w_s.at[0], sems.at[0, 0])]]
    for k in range(1, n_t):
        copies.append([
            pltpu.make_async_copy(wgot.at[j, k - 1], w_s.at[k, pl.ds(j * count, count), :], sems.at[k, j])
            for j in range(n_p)
        ])
    for per_k in copies:
        for copy in per_k:
            copy.start()
    gh[...] = dres[:half, :]
    gq[...] = dres[half:, :]
    for k in range(n_t):
        for copy in copies[k]:
            copy.wait()
        z = t_me ^ k
        wq, wk, wv = (w_s[k, i * hc : (i + 1) * hc, :] for i in range(3))
        row = lambda i: jnp.concatenate([rows0[z, i].reshape(sub, hc), rows1[z, i].reshape(sub, hc)], 0)
        gh[...] += dot(row(0), wq) + dot(row(2), wk) + dot(row(3), wv)
        gq[...] += dot(row(1), wq)


def final_proj(ti, rows0, rows1, w_own, wgot, dres):
    half = dres.shape[0] // 2
    n_t = rows0.shape[0]
    vm = pl.BlockSpec(memory_space=pltpu.VMEM)
    hbm = pl.BlockSpec(memory_space=pl.ANY)
    return pl.pallas_call(
        final_kernel,
        in_specs=[pl.BlockSpec(memory_space=pltpu.SMEM), vm, vm, hbm, hbm, vm],
        out_shape=[jax.ShapeDtypeStruct((half, D), f32)] * 2,
        scratch_shapes=[pltpu.VMEM((n_t,) + w_own.shape, bf16), pltpu.SemaphoreType.DMA((n_t, wgot.shape[0]))],
        compiler_params=pltpu.CompilerParams(vmem_limit_bytes=48 << 20),
        cost_estimate=pl.CostEstimate(flops=2 * 10**9, bytes_accessed=8 * 10**6, transcendentals=0),
        name="final_proj",
    )(ti, rows0, rows1, w_own, wgot, dres)


def unpack_kernel(pos, own, oth, gi, go, gx):
    d, c = pos[0], pos[1]
    n_d = own.shape[0]
    n_p = 2 * n_d
    n_i, n_o, n_x = gi.shape[0] // n_p, go.shape[0] // n_p, gx.shape[0] // n_p
    for j in range(n_p):
        m = d ^ (j // 2)
        piece = jnp.where(c == j % 2, own[m].astype(f32), oth[m].astype(f32))
        go[j * n_o : (j + 1) * n_o, :] = piece[:n_o]
        gi[j * n_i : (j + 1) * n_i, :] = piece[n_o : n_o + n_i]
        gx[j * n_x : (j + 1) * n_x, :] = piece[n_o + n_i :]


def unpack(pos, own, oth, n_f):
    vm = pl.BlockSpec(memory_space=pltpu.VMEM)
    sds = jax.ShapeDtypeStruct
    return pl.pallas_call(
        unpack_kernel,
        in_specs=[pl.BlockSpec(memory_space=pltpu.SMEM), vm, vm],
        out_shape=[sds((D, n_f), f32), sds((n_f, D), f32), sds((XROWS, D), f32)],
        compiler_params=pltpu.CompilerParams(vmem_limit_bytes=48 << 20),
        name="unpack",
    )(pos, own, oth)


def unpack_heads_kernel(pos, own, oth, gq, gk, gv, gr, sm):
    c = pos[1]
    hc = gq.shape[0]
    for i, g in enumerate((gq, gk, gv, gr)):
        rows = slice((i % 2) * hc, (i % 2 + 1) * hc)
        g[...] = jnp.where(c == i // 2, own[rows, :].astype(f32), oth[rows, :].astype(f32))
    sums = own[2 * hc :, :hc].astype(f32)
    sm[...] = sums[:8] + sums[8:]


def unpack_heads(pos, own, oth, hc):
    vm = pl.BlockSpec(memory_space=pltpu.VMEM)
    sds = jax.ShapeDtypeStruct
    return pl.pallas_call(
        unpack_heads_kernel,
        in_specs=[pl.BlockSpec(memory_space=pltpu.SMEM), vm, vm],
        out_shape=[sds((hc, D), f32)] * 4 + [sds((8, hc), f32)],
        compiler_params=pltpu.CompilerParams(vmem_limit_bytes=48 << 20),
        name="unpack_heads",
    )(pos, own, oth)


def table_rows(start, count):
    step = 32
    freq = 1.0 / 10000.0 ** (jnp.arange(0, D, 2).astype(f32) / D)
    coarse = (M + L - start - step * jnp.arange(count // step)).astype(f32)[:, None] * freq[None]
    fine = jnp.arange(step).astype(f32)[:, None] * freq[None]
    sin_c, cos_c = jnp.sin(coarse)[:, None], jnp.cos(coarse)[:, None]
    sin_f, cos_f = jnp.sin(fine)[None], jnp.cos(fine)[None]
    sin_a = sin_c * cos_f - cos_c * sin_f
    cos_a = cos_c * cos_f + sin_c * sin_f
    return jnp.concatenate([sin_a, cos_a], -1).reshape(count, D).astype(bf16)


def body(
    hidden, query, memory, cot_hidden, cot_query, lengths, ranks, segments,
    w_query, w_key, w_value, w_rel, w_out, bias_word, bias_rel, bias_seg, seg_embed,
    norm1_gain, norm1_bias, w_inner, b_inner, w_outer, b_outer, norm2_gain, norm2_bias,
):
    n_s, rh, _ = hidden.shape
    n_t = lax.axis_size("tensor")
    n_c = lax.axis_size("ctx")
    heads = bias_word.shape[0]
    hc = heads * DH
    n_f = w_inner.shape[1]
    rr = rh // n_t
    ci = lax.axis_index("ctx")
    ti = lax.axis_index("tensor")
    swap = [(i, (i + 1) % n_c) for i in range(n_c)]

    hid_o = lax.ppermute(hidden, "ctx", swap)
    mem_o = lax.ppermute(memory, "ctx", swap)

    n_d = lax.axis_size("dp")
    tile = 16
    di = lax.axis_index("dp")
    n_p = n_d * n_c
    while (D // n_p) % tile or (XROWS // n_p) % tile:
        n_p //= 2
    groups = n_d * n_c // n_p
    piece = (di * n_c + ci) // groups

    def across(x, k):
        return lax.ppermute(x, "tensor", [(i, i ^ k) for i in range(n_t)])

    tie = lax.optimization_barrier

    def send(own):
        return [across(own, k) for k in range(1, n_t)]

    def spread(got):
        return lax.all_gather(jnp.stack(got), ("dp", "ctx"), axis=0, tiled=False)[::groups]

    def cut(x):
        count = x.shape[0] // n_p
        return lax.dynamic_slice_in_dim(x, piece * count, count, 0)

    b_hi = b_inner.astype(bf16)
    b_lo = (b_inner - b_hi.astype(f32)).astype(bf16)
    wx = jnp.concatenate([w_out, b_hi[None], b_lo[None], jnp.zeros((XROWS - hc - 2, n_f), bf16)], 0)
    got = send(jnp.concatenate([cut(w_inner), cut(w_outer), cut(wx)], 0))
    wq, wk, wv, wr = (jnp.swapaxes(w, 0, 1) for w in (w_query, w_key, w_value, w_rel))
    w_t = jnp.concatenate([wq, wk, wv, jnp.zeros((640 - 3 * hc, D), bf16)], 0)
    ti1 = ti[None].astype(jnp.int32)
    pos = jnp.stack([di, ci, ti]).astype(jnp.int32)
    got_t = send(cut(w_t))

    table = table_rows(L - ci * rh - rh, WIN)
    wr_p = jnp.concatenate([wr, jnp.zeros((2 * LANES - hc, D), bf16)], 0)
    rk = lax.dot_general(table, wr_p, (((1,), (1,)), ((), ())), preferred_element_type=f32).astype(bf16)
    row = lambda v: jnp.pad(v.reshape(-1, hc), ((0, 0), (0, 2 * LANES - hc)))
    bw, br, bs, se = row(bias_word), row(bias_rel), row(bias_seg), row(seg_embed)

    half_s = n_s // 2
    metas = [jnp.concatenate([ci[None].astype(jnp.int32), lengths, jnp.full((1,), i * half_s, jnp.int32)]) for i in range(2)]

    def forward(meta):
        return attn_fwd(
            meta, hidden, query, memory, hid_o, mem_o, ranks, segments, wq, wk, wv, rk, bw, br, bs, se, n_t, half_s
        )

    def swap_heads(x):
        return lax.all_to_all(x, "tensor", 0, 0, tiled=True)

    att0, *kept0 = forward(metas[0])
    att0, *got = tie((att0, *got))
    wgot = spread(got)
    att_got0 = swap_heads(att0)
    meta, _ = tie((metas[1], got[0]))
    att1, *kept1 = forward(meta)
    att1, att_got0, *got_t = tie((att1, att_got0, *got_t))
    att_got1 = swap_heads(att1)
    vec1 = lambda x: x[None]
    got_t[0], _ = tie((got_t[0], wgot[0, 0, :1]))
    wgot_t = spread(got_t)
    (out_h, out_q, dres, inner, act, dpre, dout, dattn, datt0, datt1, vec, gb) = ffn(
        ti1, att_got0, att_got1, hidden, query, cot_hidden, cot_query, w_inner, w_outer, wx, wgot,
        vec1(norm1_gain), vec1(norm1_bias), vec1(b_outer), vec1(norm2_gain), vec1(norm2_bias),
    )
    datt_got0 = swap_heads(datt0)
    ga, gb_own, gb_oth = wgrad(pos, inner, act, dpre, dout, att_got0, att_got1, dattn, vec, gb, n_d)
    datt_got0, datt1, ga, gb_oth, wgot_t = tie((datt_got0, datt1, ga, gb_oth, wgot_t))
    datt_got1 = swap_heads(datt1)
    gb_got = lax.ppermute(gb_oth, "ctx", swap)
    meta, ga = tie((metas[0], ga))
    ga = lax.psum_scatter(ga, ("dp", "ctx"), scatter_dimension=0, tiled=True)[0]

    def backward(meta, kept, datt):
        p, kx, v = kept
        return attn_bwd(
            meta, p, datt, kx, v, hidden, query, memory, hid_o, mem_o, segments, wq, rk, table, bw, br, bs, se
        )

    def payload(dq, dkv_own, dkv_oth):
        dkv = (dkv_own.astype(f32) + lax.ppermute(dkv_oth, "ctx", swap).astype(f32)).astype(bf16)
        return jnp.concatenate([dq, dkv], 1)

    def along_dp(x, m):
        return lax.ppermute(x, "dp", [(i, i ^ m) for i in range(n_d)])

    def add(*terms):
        total = terms[0].astype(f32)
        for term in terms[1:]:
            total = total + term.astype(f32)
        return total.astype(bf16)

    dq, dkv_own, dkv_oth, *gw0 = backward(meta, kept0, datt_got0)
    dkv_oth, datt_got1, gb_got = tie((dkv_oth, datt_got1, gb_got))
    pay = payload(dq, dkv_own, dkv_oth)
    gb = [add(gb_own[m], gb_got[m]) for m in range(n_d)]
    meta, pay, *gb = tie((metas[1], pay, *gb))
    rows0 = swap_heads(pay)
    gb_got = [along_dp(gb[m], m) for m in range(1, n_d)]
    dq, dkv_own, dkv_oth, *gw1 = backward(meta, kept1, datt_got1)
    dkv_oth, rows0, ga, gw1[0], gw1[1], *gb_got = tie((dkv_oth, rows0, ga, gw1[0], gw1[1], *gb_got))

    gb = [add(gb[0][k], *[g[k] for g in gb_got]) for k in range(n_t)]
    ga_got = [across(ga[k], k) for k in range(1, n_t)]
    gb_got = [across(gb[k], k) for k in range(1, n_t)]
    pay = payload(dq, dkv_own, dkv_oth)
    part = add(gw0[0], gw1[0], lax.ppermute(add(gw0[1], gw1[1]), "ctx", swap))
    mask = 1
    while mask < n_d:
        part = add(part, along_dp(part, mask))
        mask *= 2
    part, pay, *got = tie((part, pay, *ga_got, *gb_got))
    ga_got, gb_got = got[: n_t - 1], got[n_t - 1 :]
    total = jnp.concatenate([add(ga[0], *ga_got), add(gb[0], *gb_got)], 0)

    pay, total, part = tie((pay, total, part))
    rows1 = swap_heads(pay)
    others = [along_dp(total, m) for m in range(1, n_d)]
    *gwt, sm = unpack_heads(pos, part, lax.ppermute(part, "ctx", swap), hc)
    gwt = [jnp.swapaxes(g, 0, 1) for g in gwt]
    rows1, *others = tie((rows1, *others))
    pieces = jnp.stack([total] + others)
    grad_h, grad_q = final_proj(ti1, rows0, rows1, w_t, wgot_t, dres)
    g_inner, g_outer, g_x = unpack(pos, pieces, lax.ppermute(pieces, "ctx", swap), n_f)
    vecs = g_x[hc + 8 : hc + 13, :hc]
    heads_of = lambda r: r.reshape(heads, DH)
    shape = (n_s, rr, D)
    return (
        out_h.reshape(shape), out_q.reshape(shape), grad_h.reshape(shape), grad_q.reshape(shape),
        gwt[0], gwt[1], gwt[2], gwt[3], g_x[:hc],
        heads_of(sm[0]), heads_of(sm[1]), heads_of(sm[2]), sm[3:5].reshape(2, heads, DH),
        vecs[0], vecs[1], g_inner, g_x[hc], g_outer,
        vecs[4], vecs[2], vecs[3],
    )


def solution(mesh):
    rows = P("dp", "ctx", None)
    by_col = P(None, "tensor")
    by_row = P("tensor", None)
    own_rows = P("dp", ("ctx", "tensor"), None)
    vec = P("tensor")
    return jax.shard_map(
        body,
        mesh=mesh,
        in_specs=(
            rows, rows, rows, rows, rows, P("dp"), P("dp", None), P("dp", None),
            by_col, by_col, by_col, by_col, by_row, by_row, by_row, by_row, P(None, "tensor", None),
            P(), P(), by_col, vec, by_row, P(), P(), P(),
        ),
        out_specs=(
            own_rows, own_rows, own_rows, own_rows,
            by_col, by_col, by_col, by_col, by_row, by_row, by_row, by_row, P(None, "tensor", None),
            vec, vec, by_col, vec, by_row, vec, vec, vec,
        ),
        check_vma=False,
    )
```

```python
from functools import partial
import math

import jax
import jax.numpy as jnp
from jax import lax
from jax.experimental import pallas as pl
from jax.experimental.pallas import tpu as pltpu
from jax.sharding import PartitionSpec as P

D = 768
DH = 64
L = 512
M = 384
KT = M + L
RQ = 256
WIN = RQ + KT
HB = 128
WB = KT + HB
LANES = 128
NEG = -1e30
EPS = 1e-12
bf16 = jnp.bfloat16
f32 = jnp.float32


def dot(a, b):
    return lax.dot_general(a, b, (((1,), (0,)), ((), ())), preferred_element_type=f32)


def dot_nt(a, b):
    return lax.dot_general(a, b, (((1,), (1,)), ((), ())), preferred_element_type=f32)


def dot_tn(a, b):
    return lax.dot_general(a, b, (((0,), (0,)), ((), ())), preferred_element_type=f32)


def iota(shape, dim):
    return lax.broadcasted_iota(jnp.int32, shape, dim)


def row_to_col(row, n):
    return jnp.transpose(jnp.broadcast_to(row, (LANES, n)))


def pad_rows(dst, src, count):
    dst[:count, :] = src
    dst[count:, :] = jnp.zeros((dst.shape[0] - count, dst.shape[1]), dst.dtype)


def seg_parts(qs, se_ref, seg_col, scale):
    d_i = iota((2 * LANES, LANES), 0)
    l_i = iota((2 * LANES, LANES), 1)
    head_of_lane = jnp.where(l_i < 8, 0, jnp.where(l_i < 16, 1, jnp.where((l_i >= 64) & (l_i < 72), 2, -1)))
    pick = ((d_i // DH) == head_of_lane).astype(bf16)
    sides = []
    for s in range(2):
        prod = qs * se_ref[s : s + 1, :] * scale
        hi = prod.astype(bf16)
        lo = (prod - hi.astype(f32)).astype(bf16)
        sides.append(dot(hi, pick) + dot(lo, pick))
    lane = iota(sides[0].shape, 1)
    val = jnp.where((lane & 3) == seg_col, sides[0], sides[1])
    hi = val.astype(bf16).astype(f32)
    lo = val - hi
    return jnp.where((lane & 7) < 4, hi, lo)


def head_mask(h, shape):
    return (iota(shape, 1) // DH) == (h & 1)


def ext_mask(h, shape):
    return (iota(shape, 1) // 8) == (h if h < 2 else 8)


def attn_fwd_kernel(
    meta, hid, qry, mem, hid_o, mem_o, ranks, segs, wq, wk, wv, rk, bw, br, bs, se,
    *rest,
):
    n_t = len(rest) - 12
    att_out = rest[:n_t]
    p_out, kx_out, v_out, wq_s, wk_s, wv_s, key_s, ma_s, word_s, rel_s, ext_s, o_s = rest[n_t:]
    t_me = meta[meta.shape[0] - 2]
    step = pl.program_id(0)
    s = step + meta[meta.shape[0] - 1]
    c = meta[0]
    length = meta[1 + s]

    @pl.when(step == 0)
    def _():
        pad_rows(wq_s, wq[...], 3 * DH)
        pad_rows(wk_s, wk[...], 3 * DH)
        pad_rows(wv_s, wv[...], 3 * DH)

    rm = mem.shape[1]
    rh = hid.shape[1]
    key_s[pl.ds(pl.multiple_of(c * rm, 64), rm), :] = mem[0]
    key_s[pl.ds(pl.multiple_of((1 - c) * rm, 64), rm), :] = mem_o[0]
    key_s[pl.ds(pl.multiple_of(M + c * rh, 64), rh), :] = hid[0]
    key_s[pl.ds(pl.multiple_of(M + (1 - c) * rh, 64), rh), :] = hid_o[0]

    seg_row = segs[pl.ds(s, 1), :]
    own_seg = jnp.where(c == 0, seg_row[:, M : M + RQ], seg_row[:, M + RQ :])
    seg_col = row_to_col(own_seg.astype(f32), RQ).astype(jnp.int32)
    rank_row = ranks[pl.ds(s, 1), :]
    own_rank = jnp.where(c == 0, rank_row[:, :RQ], rank_row[:, RQ:])
    thr_col = row_to_col(own_rank.astype(f32), RQ)[:, :1]
    valid = iota((1, L), 1) < length
    key_rank = jnp.where(valid, rank_row, 1 << 20).astype(f32)
    ma_s[0] = jnp.where(key_rank <= thr_col, 0.0, NEG)
    ma_s[1] = jnp.where(key_rank < thr_col, 0.0, NEG)

    hot = ((iota((LANES, KT), 0) & 3) == seg_row).astype(f32)
    hot = jnp.transpose(hot)
    keys = dot_nt(key_s[...], wk_s[...])
    kx_out[0, :, :LANES] = keys[:, :LANES].astype(bf16)
    kx_out[0, :, LANES : 2 * LANES] = hot.astype(bf16)
    k2 = jnp.where(iota((KT, LANES), 1) < DH, keys[:, LANES:], hot)
    kx_out[0, :, 2 * LANES :] = k2.astype(bf16)
    v_out[0] = dot_nt(key_s[...], wv_s[...]).astype(bf16)

    scale = 1.0 / math.sqrt(DH)
    for a, x_ref in enumerate((hid, qry)):
        q_raw = dot_nt(x_ref[0], wq_s[...])
        word_s[a] = ((q_raw + bw[...]) * scale).astype(bf16)
        rel_s[a] = ((q_raw + br[...]) * scale).astype(bf16)
        ext_s[a] = seg_parts(q_raw + bs[...], se, seg_col, scale).astype(bf16)

    zero_b = jnp.zeros((), bf16)
    hc = 3 * DH

    def stream(a, carry):
        outs = []
        for h in range(3):
            lo = (h // 2) * LANES
            w_h = word_s[a, :, lo : lo + LANES]
            e_h = jnp.where(ext_mask(h, (RQ, LANES)), ext_s[a], zero_b)
            if h < 2:
                qx = jnp.concatenate([jnp.where(head_mask(h, w_h.shape), w_h, zero_b), e_h], 1)
                kx = kx_out[0, :, : 2 * LANES]
            else:
                qx = jnp.where(head_mask(h, w_h.shape), w_h, e_h)
                kx = kx_out[0, :, 2 * LANES :]
            r_h = rel_s[a, :, lo : lo + LANES]
            qr = jnp.where(head_mask(h, r_h.shape), r_h, zero_b)
            content = dot_nt(qx, kx)
            for i0 in (0, HB):
                w0 = HB - i0
                pos = dot_nt(qr[i0 : i0 + HB], rk[w0 : w0 + WB, lo : lo + LANES])
                pos = pltpu.roll(pos, WB - HB, 1, stride=1, stride_axis=0)[:, :KT]
                sc = content[i0 : i0 + HB] + pos
                sc = jnp.concatenate([sc[:, :M], sc[:, M:] + ma_s[a, i0 : i0 + HB, :]], 1)
                top = jnp.max(sc, -1, keepdims=True)
                e = jnp.exp(sc - top)
                inv = 1.0 / jnp.sum(e, -1, keepdims=True)
                p_out[0, h, a, i0 : i0 + HB, :] = (e * inv).astype(bf16)
            outs.append(dot(p_out[0, h, a], v_out[0, :, lo : lo + LANES]))
        o_s[a, :, :LANES] = jnp.where(head_mask(0, outs[0].shape), outs[0], outs[1]).astype(bf16)
        o_s[a, :, LANES:] = outs[2].astype(bf16)
        return carry

    lax.fori_loop(0, 2, stream, 0)
    share_rows(att_out, lambda a, rows: o_s[a, rows, :hc], t_me)


def share_rows(dst, read, t_me):
    rr = RQ // len(dst)
    for k, ref in enumerate(dst):
        rows = pl.ds(pl.multiple_of((t_me ^ k) * rr, rr), rr)
        ref[...] = jnp.concatenate([read(0, rows), read(1, rows)], 1)


def whole(shape):
    zeros = (0,) * len(shape)
    return pl.BlockSpec(shape, lambda s, *_: zeros)


def per_seq(shape, axis=0):
    return pl.BlockSpec(shape, lambda s, *_: tuple(s if d == axis else 0 for d in range(len(shape))))


def from_seq(shape):
    return pl.BlockSpec(shape, lambda s, meta: (s + meta[meta.shape[0] - 1],) + (0,) * (len(shape) - 1))


def by_lane(shape):
    return pl.BlockSpec(shape, lambda s, *_: (0, s))


def attn_fwd(meta, hid, qry, mem, hid_o, mem_o, ranks, segs, wq, wk, wv, rk, bw, br, bs, se, n_t, count):
    _, rh, _ = hid.shape
    rm = mem.shape[1]
    hc = wq.shape[0]
    rr = rh // n_t
    seq = from_seq
    sds = jax.ShapeDtypeStruct
    grid_spec = pltpu.PrefetchScalarGridSpec(
        num_scalar_prefetch=1,
        grid=(count,),
        in_specs=[
            seq((1, rh, D)), seq((1, rh, D)), seq((1, rm, D)), seq((1, rh, D)), seq((1, rm, D)),
            whole(ranks.shape), whole(segs.shape), whole(wq.shape), whole(wk.shape), whole(wv.shape),
            whole(rk.shape), whole(bw.shape), whole(br.shape), whole(bs.shape), whole(se.shape),
        ],
        out_specs=[by_lane((rr, 2 * hc))] * n_t + [
            per_seq((1, 3, 2, rh, KT)), per_seq((1, KT, 3 * LANES)), per_seq((1, KT, 2 * LANES)),
        ],
        scratch_shapes=[
            pltpu.VMEM((2 * LANES, D), bf16), pltpu.VMEM((2 * LANES, D), bf16), pltpu.VMEM((2 * LANES, D), bf16),
            pltpu.VMEM((KT, D), bf16), pltpu.VMEM((2, RQ, L), f32), pltpu.VMEM((2, RQ, 2 * LANES), bf16),
            pltpu.VMEM((2, RQ, 2 * LANES), bf16), pltpu.VMEM((2, RQ, LANES), bf16), pltpu.VMEM((2, RQ, 2 * LANES), bf16),
        ],
    )
    out = pl.pallas_call(
        attn_fwd_kernel,
        grid_spec=grid_spec,
        out_shape=[sds((rr, count * 2 * hc), bf16)] * n_t + [
            sds((count, 3, 2, rh, KT), bf16), sds((count, KT, 3 * LANES), bf16), sds((count, KT, 2 * LANES), bf16),
        ],
        compiler_params=pltpu.CompilerParams(vmem_limit_bytes=56 << 20),
        cost_estimate=pl.CostEstimate(flops=count * 10**10, bytes_accessed=count * 16 * 10**6, transcendentals=count * 10**6),
        name="attn_fwd",
    )(meta, hid, qry, mem, hid_o, mem_o, ranks, segs, wq, wk, wv, rk, bw, br, bs, se)
    return out[:n_t], out[n_t:]


SUM_ROWS = 16


def attn_bwd_kernel(meta, p_in, kx, v, hid, qry, mem, hid_o, mem_o, segs, wq, rk, table, bw, br, bs, se, *rest):
    n_t = (len(rest) - 20) // 2
    datt, dq_out = rest[:n_t], rest[n_t : 2 * n_t]
    (dkv_own, dkv_oth, gw_own, gw_oth, wq_s, key_s, do_s, x_s, word_s, rel_s, qs_s, ds_s, sk_s, dkv_s, dw_s, dr_s, dg_s,
     g_a, gr_a, sm_a) = rest[2 * n_t :]
    t_me = meta[meta.shape[0] - 2]
    step = pl.program_id(0)
    s = step + meta[meta.shape[0] - 1]
    c = meta[0]
    rm = mem.shape[1]
    rh = hid.shape[1]
    hc = 3 * DH

    @pl.when(step == 0)
    def _():
        pad_rows(wq_s, wq[...], hc)
        do_s[:, :, hc:] = jnp.zeros((2, RQ, do_s.shape[2] - hc), bf16)
        for acc in (g_a, gr_a, sm_a):
            acc[...] = jnp.zeros(acc.shape, f32)

    key_s[pl.ds(pl.multiple_of(c * rm, 64), rm), :] = mem[0]
    key_s[pl.ds(pl.multiple_of((1 - c) * rm, 64), rm), :] = mem_o[0]
    key_s[pl.ds(pl.multiple_of(M + c * rh, 64), rh), :] = hid[0]
    key_s[pl.ds(pl.multiple_of(M + (1 - c) * rh, 64), rh), :] = hid_o[0]

    flip = (iota((RQ, RQ), 0) + iota((RQ, RQ), 1) == RQ - 1).astype(bf16)
    seg_row = segs[pl.ds(s, 1), :]
    own_seg = jnp.where(c == 0, seg_row[:, M : M + RQ], seg_row[:, M + RQ :])
    seg_col = dot(flip, row_to_col(own_seg.astype(f32), RQ).astype(bf16)).astype(jnp.int32)

    rr = RQ // n_t
    for k in range(n_t):
        rows = pl.ds(pl.multiple_of((t_me ^ k) * rr, rr), rr)
        for a in range(2):
            do_s[a, rows, :hc] = datt[k][:, a * hc : (a + 1) * hc]
    for a, x_ref in enumerate((hid, qry)):
        x_rev = dot(flip, x_ref[0]).astype(bf16)
        x_s[a] = x_rev
        q_raw = dot_nt(x_rev, wq_s[...])
        word_s[a] = (q_raw + bw[...]).astype(bf16)
        rel_s[a] = (q_raw + br[...]).astype(bf16)
        qs_s[a] = q_raw + bs[...]

    scale = 1.0 / math.sqrt(DH)
    zero_b = jnp.zeros((), bf16)
    dk_t, dv_t = [None, None], [None, None]
    lane = iota((RQ, LANES), 1)
    first_head = head_mask(0, (RQ, LANES))
    for h in range(3):
        pair = h // 2
        cols = slice(pair * LANES, (pair + 1) * LANES)
        mask2 = head_mask(h, (2 * RQ, LANES))
        kcols = slice(0, 2 * LANES) if h < 2 else slice(2 * LANES, 3 * LANES)
        base = 0 if h < 2 else 64
        own = lane - base == seg_col
        rest = (lane >= base) & (lane < base + 4) & (~own)

        def merge(dst, a, new):
            if h == 0:
                dst[a, :, cols] = new
            elif h == 1:
                dst[a, :, cols] = jnp.where(first_head, dst[a, :, cols], new)
            else:
                dst[a, :, cols] = jnp.where(first_head, new, 0.0)

        def stream(a):
            do_h = jnp.where(head_mask(h, (RQ, LANES)), do_s[a, :, cols], zero_b)
            do_r = (dot(flip, do_h) * scale).astype(bf16)
            pf = dot(flip, p_in[0, h, a])
            dp = dot_nt(do_r, v[0, :, cols])
            t = pf * dp
            delta = jnp.sum(t, -1, keepdims=True)
            ds = t - pf * delta
            ds_s[a] = ds.astype(bf16)
            for half, u0 in enumerate((0, HB)):
                blk = jnp.concatenate([ds[u0 : u0 + HB], jnp.zeros((HB, WB - KT), f32)], 1)
                sk_s[half, a] = pltpu.roll(blk, 1, 1, stride=1, stride_axis=0).astype(bf16)
            dqx = dot(ds_s[a], kx[0, :, kcols])
            side = dqx[:, LANES:] if h < 2 else dqx
            d0 = jnp.sum(jnp.where(own, side, 0.0), -1, keepdims=True)
            d1 = jnp.sum(jnp.where(rest, side, 0.0), -1, keepdims=True)
            merge(dw_s, a, dqx[:, :LANES])
            merge(dg_s, a, d0 * se[0:1, cols] + d1 * se[1:2, cols])
            qs = jnp.where(head_mask(h, (RQ, LANES)), qs_s[a, :, cols], 0.0)
            sm_a[3:4, cols] += jnp.sum(d0 * qs, 0, keepdims=True)
            sm_a[4:5, cols] += jnp.sum(d1 * qs, 0, keepdims=True)

        for a in range(2):
            stream(a)
        for half, u0 in enumerate((0, HB)):
            sk = sk_s[half].reshape(2 * HB, WB)
            dr = dot(sk, rk[u0 : u0 + WB, cols])
            for a in range(2):
                new = dr[a * HB : (a + 1) * HB]
                old = dr_s[a, u0 : u0 + HB, cols] if h == 1 else 0.0
                if h > 0:
                    hm = first_head[:HB]
                    new = jnp.where(hm, old, new) if h == 1 else jnp.where(hm, new, old)
                dr_s[a, u0 : u0 + HB, cols] = new
            r_h = jnp.concatenate([rel_s[a, u0 : u0 + HB, cols] for a in range(2)], 0)
            r_h = jnp.where(head_mask(h, r_h.shape), r_h, zero_b)
            gr_a[cols, u0 : u0 + WB] += dot_tn(r_h, sk)
        w_h = jnp.where(mask2, word_s[:, :, cols].reshape(2 * RQ, LANES), zero_b)
        part = dot_tn(w_h, ds_s[...].reshape(2 * RQ, KT))
        dk_t[pair] = part if dk_t[pair] is None else dk_t[pair] + part
        o_h = jnp.where(mask2, do_s[:, :, cols].reshape(2 * RQ, LANES), zero_b)
        part = dot_tn(o_h, p_in[0, h].reshape(2 * RQ, KT))
        dv_t[pair] = part if dv_t[pair] is None else dv_t[pair] + part

    for row, g in enumerate((dw_s, dr_s, dg_s)):
        sm_a[row : row + 1, :] += jnp.sum(g[0], 0, keepdims=True) + jnp.sum(g[1], 0, keepdims=True)
    for a in range(2):
        dq = (dw_s[a] + dr_s[a] + dg_s[a]).astype(bf16)
        g_a[0] += dot_tn(dq, x_s[a])
        do_s[a, :, :] = dot(flip, dq).astype(bf16)
    share_rows(dq_out, lambda a, rows: do_s[a, rows, :hc], t_me)
    do_s[:, :, hc:] = jnp.zeros((2, RQ, do_s.shape[2] - hc), bf16)

    for i, parts in enumerate((dk_t, dv_t)):
        g_t = jnp.concatenate(parts, 0)
        g_a[1 + i] += dot(g_t.astype(bf16), key_s[...])
        dkv_s[i] = jnp.transpose(g_t[:, M:]).astype(bf16)
    for dst, core in ((dkv_own, c), (dkv_oth, 1 - c)):
        for k in range(n_t):
            rows = pl.ds(pl.multiple_of(core * RQ + (t_me ^ k) * rr, rr), rr)
            dst[k] = jnp.concatenate([dkv_s[0, rows, :hc], dkv_s[1, rows, :hc]], 1)

    @pl.when(step == pl.num_programs(0) - 1)
    def _():
        gr = dot(gr_a[...].astype(bf16), table[...])
        for i in range(2):
            rows = slice(i * hc, (i + 1) * hc)
            last = g_a[2, :hc] if i == 0 else gr[:hc]
            first = g_a[i, :hc]
            gw_own[rows, :] = jnp.where(c == 0, first, last).astype(bf16)
            gw_oth[rows, :] = jnp.where(c == 0, last, first).astype(bf16)
        hi = sm_a[...].astype(bf16)
        lo = (sm_a[...] - hi.astype(f32)).astype(bf16)
        sums = jnp.concatenate([hi, lo], 0)
        for dst in (gw_own, gw_oth):
            dst[2 * hc :, : 2 * LANES] = sums
            dst[2 * hc :, 2 * LANES :] = jnp.zeros((SUM_ROWS, D - 2 * LANES), bf16)


def attn_bwd(meta, p, datt, kx, v, hid, qry, mem, hid_o, mem_o, segs, wq, rk, table, bw, br, bs, se):
    _, rh, _ = hid.shape
    count = p.shape[0]
    rm = mem.shape[1]
    hc = wq.shape[0]
    n_t = len(datt)
    rr = rh // n_t
    sds = jax.ShapeDtypeStruct
    g_shape = (2 * hc + SUM_ROWS, D)
    lanes = by_lane((rr, 2 * hc))
    both = pl.BlockSpec((n_t, rr, 2 * hc), lambda s, *_: (0, 0, s))
    grid_spec = pltpu.PrefetchScalarGridSpec(
        num_scalar_prefetch=1,
        grid=(count,),
        in_specs=[
            per_seq((1, 3, 2, rh, KT)), per_seq((1, KT, 3 * LANES)), per_seq((1, KT, 2 * LANES)),
            from_seq((1, rh, D)), from_seq((1, rh, D)), from_seq((1, rm, D)), from_seq((1, rh, D)), from_seq((1, rm, D)),
            whole(segs.shape), whole(wq.shape), whole(rk.shape), whole(table.shape),
            whole(bw.shape), whole(br.shape), whole(bs.shape), whole(se.shape),
        ] + [lanes] * n_t,
        out_specs=[lanes] * n_t + [both, both, whole(g_shape), whole(g_shape)],
        scratch_shapes=[
            pltpu.VMEM((2 * LANES, D), bf16), pltpu.VMEM((KT, D), bf16), pltpu.VMEM((2, RQ, 2 * LANES), bf16),
            pltpu.VMEM((2, RQ, D), bf16), pltpu.VMEM((2, RQ, 2 * LANES), bf16), pltpu.VMEM((2, RQ, 2 * LANES), bf16),
            pltpu.VMEM((2, RQ, 2 * LANES), f32), pltpu.VMEM((2, RQ, KT), bf16), pltpu.VMEM((2, 2, HB, WB), bf16),
            pltpu.VMEM((2, L, 2 * LANES), bf16), pltpu.VMEM((2, RQ, 2 * LANES), f32), pltpu.VMEM((2, RQ, 2 * LANES), f32),
            pltpu.VMEM((2, RQ, 2 * LANES), f32),
            pltpu.VMEM((3, 2 * LANES, D), f32), pltpu.VMEM((2 * LANES, WIN), f32), pltpu.VMEM((8, 2 * LANES), f32),
        ],
    )
    out = pl.pallas_call(
        attn_bwd_kernel,
        grid_spec=grid_spec,
        out_shape=[sds((rr, count * 2 * hc), bf16)] * n_t + [sds((n_t, rr, count * 2 * hc), bf16)] * 2
        + [sds(g_shape, bf16)] * 2,
        compiler_params=pltpu.CompilerParams(vmem_limit_bytes=58 << 20),
        cost_estimate=pl.CostEstimate(flops=count * 10**10, bytes_accessed=count * 16 * 10**6, transcendentals=0),
        name="attn_bwd",
    )(meta, p, kx, v, hid, qry, mem, hid_o, mem_o, segs, wq, rk, table, bw, br, bs, se, *datt)
    return out[:n_t], out[n_t], out[n_t + 1], out[n_t + 2 :]


def norm_bwd(d_out, scaled, inv_std, gain):
    e = d_out * gain
    return inv_std * (e - jnp.mean(e, -1, keepdims=True) - scaled * jnp.mean(e * scaled, -1, keepdims=True))


def norm_fwd(resid):
    cen = resid - jnp.mean(resid, -1, keepdims=True)
    inv_std = lax.rsqrt(jnp.mean(cen * cen, -1, keepdims=True) + EPS)
    return cen * inv_std, inv_std


GELU_A = 0.7978845608028654
GELU_B = 0.044715


def ffn_kernel(ti, *refs):
    n_t = (len(refs) - 47) // 4
    it = iter(refs)
    take = lambda n: [next(it) for _ in range(n)]
    att = [take(n_t) for _ in range(2)]
    (hid, qry, cot_h, cot_q, wi_own, wo_own, wx_own, wgot, n1g, n1b, bo, n2g, n2b) = take(13)
    datt_out = [take(n_t) for _ in range(2)]
    big_out = take(9)
    vec_out, gb_out = take(2)
    (wi, wo, wx, n1_s, sc1_s, inv1_s, gp_s, acc_s, dres2_s, x_s) = take(10)
    big = take(9)
    (out_h, out_q, dres_out, inner_out, act_out, dpre_out, dout_out, dattn_out, attr_out) = big
    sems, sems_x, sems_o, sems_k = take(4)
    t_me = ti[0]
    hc = attr_out.shape[2]
    rows = dres_out.shape[0]
    half = rows // 2
    n_p = wgot.shape[0]
    parts = ((wx, wx_own), (wi, wi_own), (wo, wo_own))

    def piece_copy(i, k, j):
        dst = parts[i][0]
        count = dst.shape[1] // n_p
        start = ((wi.shape[1] + wo.shape[1]) // n_p, 0, wi.shape[1] // n_p)[i]
        return pltpu.make_async_copy(
            wgot.at[j, k - 1, pl.ds(start, count), :], dst.at[k, pl.ds(j * count, count), :], sems.at[i, k, j]
        )

    copies = []
    for i, (dst, own) in enumerate(parts):
        group = [[pltpu.make_async_copy(own, dst.at[0], sems.at[i, 0, 0])]]
        group += [[piece_copy(i, k, j) for j in range(n_p)] for k in range(1, n_t)]
        copies.append(group)
    rr = x_s.shape[2]
    mine = [
        pltpu.make_async_copy(x.at[:, pl.ds(t_me * rr, rr), :], x_s.at[i], sems_x.at[i])
        for i, x in enumerate((hid, qry, cot_h, cot_q))
    ]
    for copy in mine[:2]:
        copy.start()
    for per_k in copies[0]:
        for copy in per_k:
            copy.start()
    for k in range(n_t):
        for copy in copies[1][k] + copies[2][k]:
            copy.start()
    for copy in mine[2:]:
        copy.start()
    leave = [pltpu.make_async_copy(big[i], big_out[i], sems_o.at[i]) for i in range(9)]
    leave_k = lambda i, k: pltpu.make_async_copy(big[4 + i].at[k], big_out[4 + i].at[k], sems_k.at[i, k])

    halves = (slice(0, half), slice(half, rows))
    for per_k in copies[0]:
        for copy in per_k:
            copy.wait()
    n_h = half // (2 * rr)
    for a in range(2):
        r = halves[a]
        mine[a].wait()
        acc = x_s[a].reshape(half, D).astype(f32)
        for k in range(n_t):
            pieces = [
                att[i][k][:, (2 * s + a) * hc : (2 * s + a + 1) * hc] for i in range(2) for s in range(n_h)
            ]
            part = jnp.concatenate(pieces, 0)
            attr_out[k, r, :] = part
            acc = acc + dot(part, wx[k, :hc, :])
        scaled, inv_std = norm_fwd(acc)
        sc1_s[r, :] = scaled
        inv1_s[r, :] = jnp.broadcast_to(inv_std, (half, LANES))
        n1 = scaled * n1g[...] + n1b[...]
        n1_s[r, :] = n1
        inner_out[r, :] = n1.astype(bf16)
    leave[8].start()
    leave[3].start()
    acc_s[...] = jnp.zeros(acc_s.shape, f32)

    def up(k, carry):
        @pl.when(k == 0)
        def _():
            copies[1][0][0].wait()
            copies[2][0][0].wait()

        @pl.when(k > 0)
        def _():
            for i in (1, 2):
                for j in range(n_p):
                    piece_copy(i, k, j).wait()

        bias = wx[k, hc : hc + 1, :].astype(f32) + wx[k, hc + 1 : hc + 2, :].astype(f32)
        for r in halves:
            pre = dot(inner_out[r, :], wi[k]) + bias
            sq = pre * pre
            th = jnp.tanh(GELU_A * (pre + GELU_B * (pre * sq)))
            act_out[k, r, :] = (0.5 * pre * (1.0 + th)).astype(bf16)
            gp_s[k, r, :] = 0.5 * (1.0 + th) + (0.5 * pre) * (1.0 - th * th) * (GELU_A + (3.0 * GELU_A * GELU_B) * sq)
            acc_s[r, :] += dot(act_out[k, r, :], wo[k])
        leave_k(0, k).start()
        return carry

    lax.fori_loop(0, n_t, up, 0)

    sums = [None] * 3
    for a, o_ref in enumerate((out_h, out_q)):
        r = halves[a]
        scaled, inv_std = norm_fwd(n1_s[r, :] + (acc_s[r, :] + bo[...]))
        o_ref[...] = scaled * n2g[...] + n2b[...]
        leave[a].start()
        mine[2 + a].wait()
        cot = x_s[2 + a].reshape(half, D).astype(f32)
        d2 = norm_bwd(cot, scaled, inv_std, n2g[...])
        dres2_s[r, :] = d2
        dout_out[r, :] = d2.astype(bf16)
        for i, g in enumerate((cot * scaled, cot, d2)):
            g = jnp.sum(g, 0, keepdims=True)
            sums[i] = g if a == 0 else sums[i] + g
    leave[6].start()
    vec_out[2:3, :] = sums[0]
    vec_out[3:4, :] = sums[1]
    vec_out[4:5, :] = sums[2]
    acc_s[...] = jnp.zeros(acc_s.shape, f32)

    def down(k, carry):
        total = None
        for r in halves:
            d_pre = dot_nt(dout_out[r, :], wo[k]) * gp_s[k, r, :]
            g = jnp.sum(d_pre, 0, keepdims=True)
            total = g if total is None else total + g
            dpre_out[k, r, :] = d_pre.astype(bf16)
            acc_s[r, :] += dot_nt(dpre_out[k, r, :], wi[k])
        gb_out[pl.ds(k, 1), :] = total
        leave_k(1, k).start()
        return carry

    lax.fori_loop(0, n_t, down, 0)
    for a in range(2):
        r = halves[a]
        d_n1 = dres2_s[r, :] + acc_s[r, :]
        scaled = sc1_s[r, :]
        for i, g in enumerate((d_n1 * scaled, d_n1)):
            g = jnp.sum(g, 0, keepdims=True)
            vec_out[i : i + 1, :] = g if a == 0 else vec_out[i : i + 1, :] + g
        d1 = norm_bwd(d_n1, scaled, inv1_s[r, :1], n1g[...])
        dres_out[r, :] = d1
        dattn_out[r, :] = d1.astype(bf16)
    leave[2].start()
    leave[7].start()
    for k in range(n_t):
        part = dot_nt(dattn_out[...], wx[k, :hc, :]).astype(bf16)
        for i in range(2):
            for s in range(n_h):
                first = (i * n_h + s) * rr
                datt_out[i][k][:, 2 * s * hc : (2 * s + 2) * hc] = jnp.concatenate(
                    [part[first : first + rr], part[half + first : half + first + rr]], 1
                )
    for i in (0, 1, 2, 3, 6, 7, 8):
        leave[i].wait()
    for i in range(2):
        for k in range(n_t):
            leave_k(i, k).wait()


def ffn(ti, att0, att1, hid, qry, cot_h, cot_q, w_inner, w_outer, wx_own, wgot, n1g, n1b, bo, n2g, n2b, hc):
    n_t = len(att0)
    n_f = w_outer.shape[0]
    n_s, rr = hid.shape[0], hid.shape[1] // n_t
    half = n_s * rr
    rows = 2 * half
    sds = jax.ShapeDtypeStruct
    vm = pl.BlockSpec(memory_space=pltpu.VMEM)
    hbm = pl.BlockSpec(memory_space=pl.ANY)
    big = [
        ((half, D), f32), ((half, D), f32), ((rows, D), f32), ((rows, D), bf16), ((n_t, rows, n_f), bf16),
        ((n_t, rows, n_f), bf16), ((rows, D), bf16), ((rows, D), bf16), ((n_t, rows, hc), bf16),
    ]
    out = pl.pallas_call(
        ffn_kernel,
        in_specs=[pl.BlockSpec(memory_space=pltpu.SMEM)] + [vm] * (2 * n_t) + [hbm] * 8 + [vm] * 5,
        out_specs=[vm] * (2 * n_t) + [hbm] * len(big) + [vm] * 2,
        out_shape=[sds(att0[0].shape, bf16)] * (2 * n_t) + [sds(*b) for b in big] + [sds((5, D), f32), sds((n_t, n_f), f32)],
        scratch_shapes=[
            pltpu.VMEM((n_t,) + w_inner.shape, bf16), pltpu.VMEM((n_t,) + w_outer.shape, bf16),
            pltpu.VMEM((n_t,) + wx_own.shape, bf16),
            pltpu.VMEM((rows, D), f32), pltpu.VMEM((rows, D), f32), pltpu.VMEM((rows, LANES), f32),
            pltpu.VMEM((n_t, rows, n_f), f32), pltpu.VMEM((rows, D), f32), pltpu.VMEM((rows, D), f32),
            pltpu.VMEM((4, n_s, rr, D), bf16),
        ] + [pltpu.VMEM(*b) for b in big] + [
            pltpu.SemaphoreType.DMA((3, n_t, wgot.shape[0])), pltpu.SemaphoreType.DMA((4,)),
            pltpu.SemaphoreType.DMA((len(big),)), pltpu.SemaphoreType.DMA((2, n_t)),
        ],
        compiler_params=pltpu.CompilerParams(vmem_limit_bytes=60 << 20),
        cost_estimate=pl.CostEstimate(flops=20 * 10**9, bytes_accessed=25 * 10**6, transcendentals=2 * 10**6),
        name="ffn",
    )(ti, *att0, *att1, hid, qry, cot_h, cot_q, w_inner, w_outer, wx_own, wgot, n1g, n1b, bo, n2g, n2b)
    return out[:n_t], out[n_t : 2 * n_t], out[2 * n_t : 2 * n_t + 9], out[2 * n_t + 9 :]


XROWS = 256


def wgrad_kernel(pos, inner, act, dpre, dout, attr, dattn, vec, gb, ga_out, own_out, oth_out, gx_s):
    hc = attr.shape[2]
    n_p = ga_out.shape[0]
    d, c = pos[0], pos[1]
    k = pl.program_id(0)
    z = pos[2] ^ k
    n_i, n_o, n_x = D // n_p, act.shape[2] // n_p, XROWS // n_p
    gx_s[:hc, :] = dot_tn(attr[0], dattn[...])
    gx_s[hc:, :] = jnp.zeros((gx_s.shape[0] - hc, D), f32)
    gx_s[hc : hc + 1, :] = gb[pl.ds(k, 1), :]
    for t in range(D // hc):
        @pl.when(z == t)
        def _():
            gx_s[hc + 8 : hc + 13, :hc] = vec[:, t * hc : (t + 1) * hc]
    n_a = ga_out.shape[2] - n_i
    g = dot_tn(inner[...], dpre[0]).astype(bf16)
    for j in range(n_p):
        ga_out[j, 0, :n_i] = g[j * n_i : (j + 1) * n_i]
    g = dot_tn(act[0], dout[...])
    for j in range(n_p):
        ga_out[j, 0, n_i:] = g[j * n_o : j * n_o + n_a].astype(bf16)
    for m in range(n_p // 2):
        halves = [
            jnp.concatenate([g[j * n_o + n_a : (j + 1) * n_o], gx_s[j * n_x : (j + 1) * n_x]], 0)
            for j in (2 * m, 2 * m + 1)
        ]
        own_out[m ^ d, 0] = jnp.where(c == 0, halves[0], halves[1]).astype(bf16)
        oth_out[m ^ d, 0] = jnp.where(c == 0, halves[1], halves[0]).astype(bf16)


def wgrad(pos, inner, act, dpre, dout, attr, dattn, vec, gb, n_d):
    n_t, rows, n_f = act.shape
    n_p = 2 * n_d
    n_o = n_f // n_p
    n_a = 2 * n_o // 3
    first = D // n_p + n_a
    rest = n_o - n_a + XROWS // n_p
    return pl.pallas_call(
        wgrad_kernel,
        grid=(n_t,),
        in_specs=[
            pl.BlockSpec(memory_space=pltpu.SMEM),
            whole(inner.shape), per_seq((1, rows, n_f)), per_seq((1, rows, n_f)), whole(dout.shape),
            per_seq((1,) + attr.shape[1:]), whole(dattn.shape), whole(vec.shape), whole(gb.shape),
        ],
        out_specs=[per_seq((n_p, 1, first, D), 1)] + [per_seq((n_d, 1, rest, D), 1)] * 2,
        out_shape=[
            jax.ShapeDtypeStruct((n_p, n_t, first, D), bf16)
        ] + [jax.ShapeDtypeStruct((n_d, n_t, rest, D), bf16)] * 2,
        scratch_shapes=[pltpu.VMEM((XROWS, D), f32)],
        compiler_params=pltpu.CompilerParams(vmem_limit_bytes=60 << 20),
        cost_estimate=pl.CostEstimate(flops=6 * 10**9, bytes_accessed=20 * 10**6, transcendentals=0),
        name="wgrad",
    )(pos, inner, act, dpre, dout, attr, dattn, vec, gb)


def final_kernel(*refs):
    n_t = (len(refs) - 7) // 2
    rows = (refs[:n_t], refs[n_t : 2 * n_t])
    w_own, wgot, dres, gh, gq, w_s, sems = refs[2 * n_t :]
    n_p = wgot.shape[0]
    half = gh.shape[0]
    rr = rows[0][0].shape[0] // 2
    n_h = half // (2 * rr)
    hc = rows[0][0].shape[1] // (2 * n_h)
    count = wgot.shape[2]
    copies = [[pltpu.make_async_copy(w_own, w_s.at[0], sems.at[0, 0])]]
    for k in range(1, n_t):
        copies.append([
            pltpu.make_async_copy(wgot.at[j, k - 1], w_s.at[k, pl.ds(j * count, count), :], sems.at[k, j])
            for j in range(n_p)
        ])
    for per_k in copies:
        for copy in per_k:
            copy.start()
    gh[...] = dres[:half, :]
    gq[...] = dres[half:, :]
    for k in range(n_t):
        for copy in copies[k]:
            copy.wait()
        wq, wk, wv = (w_s[k, i * hc : (i + 1) * hc, :] for i in range(3))

        def kind(low, i):
            return jnp.concatenate([
                rows[side][k][low : low + rr, (2 * s + i) * hc : (2 * s + i + 1) * hc]
                for side in range(2) for s in range(n_h)
            ], 0)

        gh[...] += dot(kind(0, 0), wq) + dot(kind(rr, 0), wk) + dot(kind(rr, 1), wv)
        gq[...] += dot(kind(0, 1), wq)


def final_proj(rows0, rows1, w_own, wgot, dres):
    half = dres.shape[0] // 2
    n_t = len(rows0)
    vm = pl.BlockSpec(memory_space=pltpu.VMEM)
    hbm = pl.BlockSpec(memory_space=pl.ANY)
    return pl.pallas_call(
        final_kernel,
        in_specs=[vm] * (2 * n_t) + [hbm, hbm, vm],
        out_shape=[jax.ShapeDtypeStruct((half, D), f32)] * 2,
        scratch_shapes=[pltpu.VMEM((n_t,) + w_own.shape, bf16), pltpu.SemaphoreType.DMA((n_t, wgot.shape[0]))],
        compiler_params=pltpu.CompilerParams(vmem_limit_bytes=48 << 20),
        cost_estimate=pl.CostEstimate(flops=2 * 10**9, bytes_accessed=8 * 10**6, transcendentals=0),
        name="final_proj",
    )(*rows0, *rows1, w_own, wgot, dres)


def unpack_kernel(pos, own, oth, gi, go, gx, gi_s, go_s, gx_s, sems):
    d, c = pos[0], pos[1]
    n_d = own.shape[0]
    n_p = 2 * n_d
    n_i, n_o, n_x = gi_s.shape[0] // n_p, go_s.shape[0] // n_p, gx_s.shape[0] // n_p
    copies = []
    for j in range(n_p):
        m = d ^ (j // 2)
        piece = jnp.where(c == j % 2, own[m].astype(f32), oth[m].astype(f32))
        parts = ((gi_s, gi, n_i, 0), (go_s, go, n_o, n_i), (gx_s, gx, n_x, n_i + n_o))
        for i, (src, dst, count, first) in enumerate(parts):
            rows = slice(j * count, (j + 1) * count)
            src[rows, :] = piece[first : first + count]
            copies.append(pltpu.make_async_copy(src.at[rows, :], dst.at[rows, :], sems.at[i, j]))
            copies[-1].start()
    for copy in copies:
        copy.wait()


def unpack(pos, own, oth, n_f):
    vm = pl.BlockSpec(memory_space=pltpu.VMEM)
    hbm = pl.BlockSpec(memory_space=pl.ANY)
    shapes = [(D, n_f), (n_f, D), (XROWS, D)]
    return pl.pallas_call(
        unpack_kernel,
        in_specs=[pl.BlockSpec(memory_space=pltpu.SMEM), vm, vm],
        out_specs=[hbm] * 3,
        out_shape=[jax.ShapeDtypeStruct(shape, f32) for shape in shapes],
        scratch_shapes=[pltpu.VMEM(shape, f32) for shape in shapes] + [pltpu.SemaphoreType.DMA((3, 2 * own.shape[0]))],
        compiler_params=pltpu.CompilerParams(vmem_limit_bytes=48 << 20),
        name="unpack",
    )(pos, own, oth)


def unpack_heads_kernel(pos, own, oth, gq, gk, gv, gr, sm):
    c = pos[1]
    hc = gq.shape[0]
    for i, g in enumerate((gq, gk, gv, gr)):
        rows = slice((i % 2) * hc, (i % 2 + 1) * hc)
        g[...] = jnp.where(c == i // 2, own[rows, :].astype(f32), oth[rows, :].astype(f32))
    sums = own[2 * hc :, :hc].astype(f32)
    sm[...] = sums[:8] + sums[8:]


def unpack_heads(pos, own, oth, hc):
    vm = pl.BlockSpec(memory_space=pltpu.VMEM)
    sds = jax.ShapeDtypeStruct
    return pl.pallas_call(
        unpack_heads_kernel,
        in_specs=[pl.BlockSpec(memory_space=pltpu.SMEM), vm, vm],
        out_shape=[sds((hc, D), f32)] * 4 + [sds((8, hc), f32)],
        compiler_params=pltpu.CompilerParams(vmem_limit_bytes=48 << 20),
        name="unpack_heads",
    )(pos, own, oth)


def table_rows(start, count):
    step = 32
    freq = 1.0 / 10000.0 ** (jnp.arange(0, D, 2).astype(f32) / D)
    coarse = (M + L - start - step * jnp.arange(count // step)).astype(f32)[:, None] * freq[None]
    fine = jnp.arange(step).astype(f32)[:, None] * freq[None]
    sin_c, cos_c = jnp.sin(coarse)[:, None], jnp.cos(coarse)[:, None]
    sin_f, cos_f = jnp.sin(fine)[None], jnp.cos(fine)[None]
    sin_a = sin_c * cos_f - cos_c * sin_f
    cos_a = cos_c * cos_f + sin_c * sin_f
    return jnp.concatenate([sin_a, cos_a], -1).reshape(count, D).astype(bf16)


def body(
    hidden, query, memory, cot_hidden, cot_query, lengths, ranks, segments,
    w_query, w_key, w_value, w_rel, w_out, bias_word, bias_rel, bias_seg, seg_embed,
    norm1_gain, norm1_bias, w_inner, b_inner, w_outer, b_outer, norm2_gain, norm2_bias,
):
    n_s, rh, _ = hidden.shape
    n_t = lax.axis_size("tensor")
    n_c = lax.axis_size("ctx")
    heads = bias_word.shape[0]
    hc = heads * DH
    n_f = w_inner.shape[1]
    rr = rh // n_t
    ci = lax.axis_index("ctx")
    ti = lax.axis_index("tensor")
    swap = [(i, (i + 1) % n_c) for i in range(n_c)]

    hid_o = lax.ppermute(hidden, "ctx", swap)
    mem_o = lax.ppermute(memory, "ctx", swap)

    n_d = lax.axis_size("dp")
    tile = 16
    di = lax.axis_index("dp")
    n_p = n_d * n_c
    while (D // n_p) % tile or (XROWS // n_p) % tile:
        n_p //= 2
    groups = n_d * n_c // n_p
    piece = (di * n_c + ci) // groups

    def across(x, k):
        return lax.ppermute(x, "tensor", [(i, i ^ k) for i in range(n_t)])

    tie = lax.optimization_barrier

    def send(own):
        return [across(own, k) for k in range(1, n_t)]

    def spread(got):
        return lax.all_gather(jnp.stack(got), ("dp", "ctx"), axis=0, tiled=False)[::groups]

    def cut(x):
        count = x.shape[0] // n_p
        return lax.dynamic_slice_in_dim(x, piece * count, count, 0)

    b_hi = b_inner.astype(bf16)
    b_lo = (b_inner - b_hi.astype(f32)).astype(bf16)
    wx = jnp.concatenate([w_out, b_hi[None], b_lo[None], jnp.zeros((XROWS - hc - 2, n_f), bf16)], 0)
    got = send(jnp.concatenate([cut(w_inner), cut(w_outer), cut(wx)], 0))
    wq, wk, wv, wr = (jnp.swapaxes(w, 0, 1) for w in (w_query, w_key, w_value, w_rel))
    w_t = jnp.concatenate([wq, wk, wv, jnp.zeros((640 - 3 * hc, D), bf16)], 0)
    ti1 = ti[None].astype(jnp.int32)
    pos = jnp.stack([di, ci, ti]).astype(jnp.int32)
    got_t = send(cut(w_t))

    table = table_rows(L - ci * rh - rh, WIN)
    wr_p = jnp.concatenate([wr, jnp.zeros((2 * LANES - hc, D), bf16)], 0)
    rk = lax.dot_general(table, wr_p, (((1,), (1,)), ((), ())), preferred_element_type=f32).astype(bf16)
    row = lambda v: jnp.pad(v.reshape(-1, hc), ((0, 0), (0, 2 * LANES - hc)))
    bw, br, bs, se = row(bias_word), row(bias_rel), row(bias_seg), row(seg_embed)

    half_s = n_s // 2
    metas = [
        jnp.concatenate([ci[None].astype(jnp.int32), lengths, ti1, jnp.full((1,), i * half_s, jnp.int32)]) for i in range(2)
    ]

    def forward(meta):
        return attn_fwd(
            meta, hidden, query, memory, hid_o, mem_o, ranks, segments, wq, wk, wv, rk, bw, br, bs, se, n_t, half_s
        )

    def share(own):
        return [own[0]] + [across(own[k], k) for k in range(1, n_t)]

    def along_dp(x, m):
        return lax.ppermute(x, "dp", [(i, i ^ m) for i in range(n_d)])

    def add(*terms):
        total = terms[0].astype(f32)
        for term in terms[1:]:
            total = total + term.astype(f32)
        return total.astype(bf16)

    def tie_all(*groups):
        flat = tie(tuple(x for group in groups for x in group))
        out, first = [], 0
        for group in groups:
            out.append(list(flat[first : first + len(group)]))
            first += len(group)
        return out

    att0, kept0 = forward(metas[0])
    att0, got = tie_all(att0, got)
    wgot = spread(got)
    att0 = share(att0)
    meta, _ = tie((metas[1], got[0]))
    att1, kept1 = forward(meta)
    att1, att0, got_t = tie_all(att1, att0, got_t)
    att1 = share(att1)
    vec1 = lambda x: x[None]
    got_t[0], _ = tie((got_t[0], wgot[0, 0, :1]))
    wgot_t = spread(got_t)
    datt0, datt1, big, (vec, gb) = ffn(
        ti1, att0, att1, hidden, query, cot_hidden, cot_query, w_inner, w_outer, wx, wgot,
        vec1(norm1_gain), vec1(norm1_bias), vec1(b_outer), vec1(norm2_gain), vec1(norm2_bias), hc,
    )
    out_h, out_q, dres, inner, act, dpre, dout, dattn, attr = big
    datt0 = share(datt0)
    ga, gb_own, gb_oth = wgrad(pos, inner, act, dpre, dout, attr, dattn, vec, gb, n_d)
    datt0, datt1, (ga, gb_oth, wgot_t) = tie_all(datt0, datt1, [ga, gb_oth, wgot_t])
    datt1 = share(datt1)
    gb_got = lax.ppermute(gb_oth, "ctx", swap)
    meta, ga = tie((metas[0], ga))
    ga = lax.psum_scatter(ga, ("dp", "ctx"), scatter_dimension=0, tiled=True)[0]

    def backward(meta, kept, datt):
        p, kx, v = kept
        return attn_bwd(
            meta, p, datt, kx, v, hidden, query, memory, hid_o, mem_o, segments, wq, rk, table, bw, br, bs, se
        )

    def payload(dq, dkv_own, dkv_oth):
        got = lax.ppermute(dkv_oth, "ctx", swap)
        return [jnp.concatenate([dq[k], add(dkv_own[k], got[k])], 0) for k in range(n_t)]

    dq, dkv_own, dkv_oth, gw0 = backward(meta, kept0, datt0)
    (dkv_oth, gb_got), datt1 = tie_all([dkv_oth, gb_got], datt1)
    pay = payload(dq, dkv_own, dkv_oth)
    gb = [add(gb_own[m], gb_got[m]) for m in range(n_d)]
    (meta,), pay, gb = tie_all([metas[1]], pay, gb)
    rows0 = share(pay)
    gb_got = [along_dp(gb[m], m) for m in range(1, n_d)]
    dq, dkv_own, dkv_oth, gw1 = backward(meta, kept1, datt1)
    (dkv_oth, ga), rows0, gw1, gb_got = tie_all([dkv_oth, ga], rows0, gw1, gb_got)

    total = [jnp.concatenate([ga[k], add(gb[0][k], *[g[k] for g in gb_got])], 0) for k in range(n_t)]
    total_got = [across(total[k], k) for k in range(1, n_t)]
    pay = payload(dq, dkv_own, dkv_oth)
    part = add(gw0[0], gw1[0], lax.ppermute(add(gw0[1], gw1[1]), "ctx", swap))
    mask = 1
    while mask < n_d:
        part = add(part, along_dp(part, mask))
        mask *= 2
    (part,), pay, total_got = tie_all([part], pay, total_got)
    total = add(total[0], *total_got)

    pay, (total, part) = tie_all(pay, [total, part])
    rows1 = share(pay)
    others = [along_dp(total, m) for m in range(1, n_d)]
    *gwt, sm = unpack_heads(pos, part, lax.ppermute(part, "ctx", swap), hc)
    gwt = [jnp.swapaxes(g, 0, 1) for g in gwt]
    rows1, others = tie_all(rows1, others)
    pieces = jnp.stack([total] + others)
    grad_h, grad_q = final_proj(rows0, rows1, w_t, wgot_t, dres)
    g_inner, g_outer, g_x = unpack(pos, pieces, lax.ppermute(pieces, "ctx", swap), n_f)
    vecs = g_x[hc + 8 : hc + 13, :hc]
    heads_of = lambda r: r.reshape(heads, DH)
    shape = (n_s, rr, D)
    return (
        out_h.reshape(shape), out_q.reshape(shape), grad_h.reshape(shape), grad_q.reshape(shape),
        gwt[0], gwt[1], gwt[2], gwt[3], g_x[:hc],
        heads_of(sm[0]), heads_of(sm[1]), heads_of(sm[2]), sm[3:5].reshape(2, heads, DH),
        vecs[0], vecs[1], g_inner, g_x[hc], g_outer,
        vecs[4], vecs[2], vecs[3],
    )


def solution(mesh):
    rows = P("dp", "ctx", None)
    by_col = P(None, "tensor")
    by_row = P("tensor", None)
    own_rows = P("dp", ("ctx", "tensor"), None)
    vec = P("tensor")
    return jax.shard_map(
        body,
        mesh=mesh,
        in_specs=(
            rows, rows, rows, rows, rows, P("dp"), P("dp", None), P("dp", None),
            by_col, by_col, by_col, by_col, by_row, by_row, by_row, by_row, P(None, "tensor", None),
            P(), P(), by_col, vec, by_row, P(), P(), P(),
        ),
        out_specs=(
            own_rows, own_rows, own_rows, own_rows,
            by_col, by_col, by_col, by_col, by_row, by_row, by_row, by_row, P(None, "tensor", None),
            vec, vec, by_col, vec, by_row, vec, vec, vec,
        ),
        check_vma=False,
    )
```

```python
from functools import partial
import math

import jax
import jax.numpy as jnp
from jax import lax
from jax.experimental import pallas as pl
from jax.experimental.pallas import tpu as pltpu
from jax.sharding import PartitionSpec as P

D = 768
DH = 64
L = 512
M = 384
KT = M + L
RQ = 256
WIN = RQ + KT
HB = 128
WB = KT + HB
LANES = 128
NEG = -1e30
EPS = 1e-12
bf16 = jnp.bfloat16
f32 = jnp.float32


def dot(a, b):
    return lax.dot_general(a, b, (((1,), (0,)), ((), ())), preferred_element_type=f32)


def dot_nt(a, b):
    return lax.dot_general(a, b, (((1,), (1,)), ((), ())), preferred_element_type=f32)


def dot_tn(a, b):
    return lax.dot_general(a, b, (((0,), (0,)), ((), ())), preferred_element_type=f32)


def iota(shape, dim):
    return lax.broadcasted_iota(jnp.int32, shape, dim)


def row_to_col(row, n):
    return jnp.transpose(jnp.broadcast_to(row, (LANES, n)))


def pad_rows(dst, src, count):
    dst[:count, :] = src
    dst[count:, :] = jnp.zeros((dst.shape[0] - count, dst.shape[1]), dst.dtype)


def seg_parts(qs, se_ref, seg_col, scale):
    d_i = iota((2 * LANES, LANES), 0)
    l_i = iota((2 * LANES, LANES), 1)
    head_of_lane = jnp.where(l_i < 8, 0, jnp.where(l_i < 16, 1, jnp.where((l_i >= 64) & (l_i < 72), 2, -1)))
    pick = ((d_i // DH) == head_of_lane).astype(bf16)
    sides = []
    for s in range(2):
        prod = qs * se_ref[s : s + 1, :] * scale
        hi = prod.astype(bf16)
        lo = (prod - hi.astype(f32)).astype(bf16)
        sides.append(dot(hi, pick) + dot(lo, pick))
    lane = iota(sides[0].shape, 1)
    val = jnp.where((lane & 3) == seg_col, sides[0], sides[1])
    hi = val.astype(bf16).astype(f32)
    lo = val - hi
    return jnp.where((lane & 7) < 4, hi, lo)


def head_mask(h, shape):
    return (iota(shape, 1) // DH) == (h & 1)


def ext_mask(h, shape):
    return (iota(shape, 1) // 8) == (h if h < 2 else 8)


def attn_fwd_kernel(
    meta, hid, qry, mem, hid_o, mem_o, ranks, segs, wq, wk, wv, rk, bw, br, bs, se,
    *rest,
):
    n_t = len(rest) - 12
    att_out = rest[:n_t]
    p_out, kx_out, v_out, wq_s, wk_s, wv_s, key_s, ma_s, word_s, rel_s, ext_s, o_s = rest[n_t:]
    t_me = meta[meta.shape[0] - 2]
    step = pl.program_id(0)
    s = step + meta[meta.shape[0] - 1]
    c = meta[0]
    length = meta[1 + s]

    @pl.when(step == 0)
    def _():
        pad_rows(wq_s, wq[...], 3 * DH)
        pad_rows(wk_s, wk[...], 3 * DH)
        pad_rows(wv_s, wv[...], 3 * DH)

    rm = mem.shape[1]
    rh = hid.shape[1]
    key_s[pl.ds(pl.multiple_of(c * rm, 64), rm), :] = mem[0]
    key_s[pl.ds(pl.multiple_of((1 - c) * rm, 64), rm), :] = mem_o[0]
    key_s[pl.ds(pl.multiple_of(M + c * rh, 64), rh), :] = hid[0]
    key_s[pl.ds(pl.multiple_of(M + (1 - c) * rh, 64), rh), :] = hid_o[0]

    seg_row = segs[pl.ds(s, 1), :]
    own_seg = jnp.where(c == 0, seg_row[:, M : M + RQ], seg_row[:, M + RQ :])
    seg_col = row_to_col(own_seg.astype(f32), RQ).astype(jnp.int32)
    rank_row = ranks[pl.ds(s, 1), :]
    own_rank = jnp.where(c == 0, rank_row[:, :RQ], rank_row[:, RQ:])
    thr_col = row_to_col(own_rank.astype(f32), RQ)[:, :1]
    valid = iota((1, L), 1) < length
    key_rank = jnp.where(valid, rank_row, 1 << 20).astype(f32)
    ma_s[0] = jnp.where(key_rank <= thr_col, 0.0, NEG)
    ma_s[1] = jnp.where(key_rank < thr_col, 0.0, NEG)

    hot = ((iota((LANES, KT), 0) & 3) == seg_row).astype(f32)
    hot = jnp.transpose(hot)
    keys = dot_nt(key_s[...], wk_s[...])
    kx_out[0, :, :LANES] = keys[:, :LANES].astype(bf16)
    kx_out[0, :, LANES : 2 * LANES] = hot.astype(bf16)
    k2 = jnp.where(iota((KT, LANES), 1) < DH, keys[:, LANES:], hot)
    kx_out[0, :, 2 * LANES :] = k2.astype(bf16)
    v_out[0] = dot_nt(key_s[...], wv_s[...]).astype(bf16)

    scale = 1.0 / math.sqrt(DH)
    for a, x_ref in enumerate((hid, qry)):
        q_raw = dot_nt(x_ref[0], wq_s[...])
        word_s[a] = ((q_raw + bw[...]) * scale).astype(bf16)
        rel_s[a] = ((q_raw + br[...]) * scale).astype(bf16)
        ext_s[a] = seg_parts(q_raw + bs[...], se, seg_col, scale).astype(bf16)

    zero_b = jnp.zeros((), bf16)
    hc = 3 * DH

    def stream(a, carry):
        outs = []
        for h in range(3):
            lo = (h // 2) * LANES
            w_h = word_s[a, :, lo : lo + LANES]
            e_h = jnp.where(ext_mask(h, (RQ, LANES)), ext_s[a], zero_b)
            if h < 2:
                qx = jnp.concatenate([jnp.where(head_mask(h, w_h.shape), w_h, zero_b), e_h], 1)
                kx = kx_out[0, :, : 2 * LANES]
            else:
                qx = jnp.where(head_mask(h, w_h.shape), w_h, e_h)
                kx = kx_out[0, :, 2 * LANES :]
            r_h = rel_s[a, :, lo : lo + LANES]
            qr = jnp.where(head_mask(h, r_h.shape), r_h, zero_b)
            content = dot_nt(qx, kx)
            for i0 in (0, HB):
                w0 = HB - i0
                pos = dot_nt(qr[i0 : i0 + HB], rk[w0 : w0 + WB, lo : lo + LANES])
                pos = pltpu.roll(pos, WB - HB, 1, stride=1, stride_axis=0)[:, :KT]
                sc = content[i0 : i0 + HB] + pos
                sc = jnp.concatenate([sc[:, :M], sc[:, M:] + ma_s[a, i0 : i0 + HB, :]], 1)
                top = jnp.max(sc, -1, keepdims=True)
                e = jnp.exp(sc - top)
                inv = 1.0 / jnp.sum(e, -1, keepdims=True)
                p_out[0, h, a, i0 : i0 + HB, :] = (e * inv).astype(bf16)
            outs.append(dot(p_out[0, h, a], v_out[0, :, lo : lo + LANES]))
        o_s[a, :, :LANES] = jnp.where(head_mask(0, outs[0].shape), outs[0], outs[1]).astype(bf16)
        o_s[a, :, LANES:] = outs[2].astype(bf16)
        return carry

    lax.fori_loop(0, 2, stream, 0)
    share_rows(att_out, lambda a, rows: o_s[a, rows, :hc], t_me)


def share_rows(dst, read, t_me):
    rr = RQ // len(dst)
    for k, ref in enumerate(dst):
        rows = pl.ds(pl.multiple_of((t_me ^ k) * rr, rr), rr)
        ref[...] = jnp.concatenate([read(0, rows), read(1, rows)], 1)


def whole(shape):
    zeros = (0,) * len(shape)
    return pl.BlockSpec(shape, lambda s, *_: zeros)


def per_seq(shape, axis=0):
    return pl.BlockSpec(shape, lambda s, *_: tuple(s if d == axis else 0 for d in range(len(shape))))


def from_seq(shape):
    return pl.BlockSpec(shape, lambda s, meta: (s + meta[meta.shape[0] - 1],) + (0,) * (len(shape) - 1))


def by_lane(shape):
    return pl.BlockSpec(shape, lambda s, *_: (0, s))


def attn_fwd(meta, hid, qry, mem, hid_o, mem_o, ranks, segs, wq, wk, wv, rk, bw, br, bs, se, n_t, count):
    _, rh, _ = hid.shape
    rm = mem.shape[1]
    hc = wq.shape[0]
    rr = rh // n_t
    seq = from_seq
    sds = jax.ShapeDtypeStruct
    grid_spec = pltpu.PrefetchScalarGridSpec(
        num_scalar_prefetch=1,
        grid=(count,),
        in_specs=[
            seq((1, rh, D)), seq((1, rh, D)), seq((1, rm, D)), seq((1, rh, D)), seq((1, rm, D)),
            whole(ranks.shape), whole(segs.shape), whole(wq.shape), whole(wk.shape), whole(wv.shape),
            whole(rk.shape), whole(bw.shape), whole(br.shape), whole(bs.shape), whole(se.shape),
        ],
        out_specs=[by_lane((rr, 2 * hc))] * n_t + [
            per_seq((1, 3, 2, rh, KT)), per_seq((1, KT, 3 * LANES)), per_seq((1, KT, 2 * LANES)),
        ],
        scratch_shapes=[
            pltpu.VMEM((2 * LANES, D), bf16), pltpu.VMEM((2 * LANES, D), bf16), pltpu.VMEM((2 * LANES, D), bf16),
            pltpu.VMEM((KT, D), bf16), pltpu.VMEM((2, RQ, L), f32), pltpu.VMEM((2, RQ, 2 * LANES), bf16),
            pltpu.VMEM((2, RQ, 2 * LANES), bf16), pltpu.VMEM((2, RQ, LANES), bf16), pltpu.VMEM((2, RQ, 2 * LANES), bf16),
        ],
    )
    out = pl.pallas_call(
        attn_fwd_kernel,
        grid_spec=grid_spec,
        out_shape=[sds((rr, count * 2 * hc), bf16)] * n_t + [
            sds((count, 3, 2, rh, KT), bf16), sds((count, KT, 3 * LANES), bf16), sds((count, KT, 2 * LANES), bf16),
        ],
        compiler_params=pltpu.CompilerParams(vmem_limit_bytes=56 << 20),
        cost_estimate=pl.CostEstimate(flops=count * 10**10, bytes_accessed=count * 16 * 10**6, transcendentals=count * 10**6),
        name="attn_fwd",
    )(meta, hid, qry, mem, hid_o, mem_o, ranks, segs, wq, wk, wv, rk, bw, br, bs, se)
    return out[:n_t], out[n_t:]


SUM_ROWS = 16


def attn_bwd_kernel(meta, p_in, kx, v, hid, qry, mem, hid_o, mem_o, segs, wq, rk, table, bw, br, bs, se, *rest):
    n_t = (len(rest) - 20) // 2
    datt, dq_out = rest[:n_t], rest[n_t : 2 * n_t]
    (dkv_own, dkv_oth, gw_own, gw_oth, wq_s, key_s, do_s, x_s, word_s, rel_s, qs_s, ds_s, sk_s, dkv_s, dw_s, dr_s, dg_s,
     g_a, gr_a, sm_a) = rest[2 * n_t :]
    t_me = meta[meta.shape[0] - 2]
    step = pl.program_id(0)
    s = step + meta[meta.shape[0] - 1]
    c = meta[0]
    rm = mem.shape[1]
    rh = hid.shape[1]
    hc = 3 * DH

    @pl.when(step == 0)
    def _():
        pad_rows(wq_s, wq[...], hc)
        do_s[:, :, hc:] = jnp.zeros((2, RQ, do_s.shape[2] - hc), bf16)
        for acc in (g_a, gr_a, sm_a):
            acc[...] = jnp.zeros(acc.shape, f32)

    key_s[pl.ds(pl.multiple_of(c * rm, 64), rm), :] = mem[0]
    key_s[pl.ds(pl.multiple_of((1 - c) * rm, 64), rm), :] = mem_o[0]
    key_s[pl.ds(pl.multiple_of(M + c * rh, 64), rh), :] = hid[0]
    key_s[pl.ds(pl.multiple_of(M + (1 - c) * rh, 64), rh), :] = hid_o[0]

    flip = (iota((RQ, RQ), 0) + iota((RQ, RQ), 1) == RQ - 1).astype(bf16)
    seg_row = segs[pl.ds(s, 1), :]
    own_seg = jnp.where(c == 0, seg_row[:, M : M + RQ], seg_row[:, M + RQ :])
    seg_col = dot(flip, row_to_col(own_seg.astype(f32), RQ).astype(bf16)).astype(jnp.int32)

    rr = RQ // n_t
    for k in range(n_t):
        rows = pl.ds(pl.multiple_of((t_me ^ k) * rr, rr), rr)
        for a in range(2):
            do_s[a, rows, :hc] = datt[k][:, a * hc : (a + 1) * hc]
    for a, x_ref in enumerate((hid, qry)):
        x_rev = dot(flip, x_ref[0]).astype(bf16)
        x_s[a] = x_rev
        q_raw = dot_nt(x_rev, wq_s[...])
        word_s[a] = (q_raw + bw[...]).astype(bf16)
        rel_s[a] = (q_raw + br[...]).astype(bf16)
        qs_s[a] = q_raw + bs[...]

    scale = 1.0 / math.sqrt(DH)
    zero_b = jnp.zeros((), bf16)
    dk_t, dv_t = [None, None], [None, None]
    lane = iota((RQ, LANES), 1)
    first_head = head_mask(0, (RQ, LANES))
    for h in range(3):
        pair = h // 2
        cols = slice(pair * LANES, (pair + 1) * LANES)
        mask2 = head_mask(h, (2 * RQ, LANES))
        kcols = slice(0, 2 * LANES) if h < 2 else slice(2 * LANES, 3 * LANES)
        base = 0 if h < 2 else 64
        own = lane - base == seg_col
        rest = (lane >= base) & (lane < base + 4) & (~own)

        def merge(dst, a, new):
            if h == 0:
                dst[a, :, cols] = new
            elif h == 1:
                dst[a, :, cols] = jnp.where(first_head, dst[a, :, cols], new)
            else:
                dst[a, :, cols] = jnp.where(first_head, new, 0.0)

        def stream(a):
            do_h = jnp.where(head_mask(h, (RQ, LANES)), do_s[a, :, cols], zero_b)
            do_r = (dot(flip, do_h) * scale).astype(bf16)
            pf = dot(flip, p_in[0, h, a])
            dp = dot_nt(do_r, v[0, :, cols])
            t = pf * dp
            delta = jnp.sum(t, -1, keepdims=True)
            ds = t - pf * delta
            ds_s[a] = ds.astype(bf16)
            for half, u0 in enumerate((0, HB)):
                blk = jnp.concatenate([ds[u0 : u0 + HB], jnp.zeros((HB, WB - KT), f32)], 1)
                sk_s[half, a] = pltpu.roll(blk, 1, 1, stride=1, stride_axis=0).astype(bf16)
            dqx = dot(ds_s[a], kx[0, :, kcols])
            side = dqx[:, LANES:] if h < 2 else dqx
            d0 = jnp.sum(jnp.where(own, side, 0.0), -1, keepdims=True)
            d1 = jnp.sum(jnp.where(rest, side, 0.0), -1, keepdims=True)
            merge(dw_s, a, dqx[:, :LANES])
            merge(dg_s, a, d0 * se[0:1, cols] + d1 * se[1:2, cols])
            qs = jnp.where(head_mask(h, (RQ, LANES)), qs_s[a, :, cols], 0.0)
            sm_a[3:4, cols] += jnp.sum(d0 * qs, 0, keepdims=True)
            sm_a[4:5, cols] += jnp.sum(d1 * qs, 0, keepdims=True)

        for a in range(2):
            stream(a)
        for half, u0 in enumerate((0, HB)):
            sk = sk_s[half].reshape(2 * HB, WB)
            dr = dot(sk, rk[u0 : u0 + WB, cols])
            for a in range(2):
                new = dr[a * HB : (a + 1) * HB]
                old = dr_s[a, u0 : u0 + HB, cols] if h == 1 else 0.0
                if h > 0:
                    hm = first_head[:HB]
                    new = jnp.where(hm, old, new) if h == 1 else jnp.where(hm, new, old)
                dr_s[a, u0 : u0 + HB, cols] = new
            r_h = jnp.concatenate([rel_s[a, u0 : u0 + HB, cols] for a in range(2)], 0)
            r_h = jnp.where(head_mask(h, r_h.shape), r_h, zero_b)
            gr_a[cols, u0 : u0 + WB] += dot_tn(r_h, sk)
        w_h = jnp.where(mask2, word_s[:, :, cols].reshape(2 * RQ, LANES), zero_b)
        part = dot_tn(w_h, ds_s[...].reshape(2 * RQ, KT))
        dk_t[pair] = part if dk_t[pair] is None else dk_t[pair] + part
        o_h = jnp.where(mask2, do_s[:, :, cols].reshape(2 * RQ, LANES), zero_b)
        part = dot_tn(o_h, p_in[0, h].reshape(2 * RQ, KT))
        dv_t[pair] = part if dv_t[pair] is None else dv_t[pair] + part

    for row, g in enumerate((dw_s, dr_s, dg_s)):
        sm_a[row : row + 1, :] += jnp.sum(g[0], 0, keepdims=True) + jnp.sum(g[1], 0, keepdims=True)
    for a in range(2):
        dq = (dw_s[a] + dr_s[a] + dg_s[a]).astype(bf16)
        g_a[0] += dot_tn(dq, x_s[a])
        do_s[a, :, :] = dot(flip, dq).astype(bf16)
    share_rows(dq_out, lambda a, rows: do_s[a, rows, :hc], t_me)
    do_s[:, :, hc:] = jnp.zeros((2, RQ, do_s.shape[2] - hc), bf16)

    for i, parts in enumerate((dk_t, dv_t)):
        g_t = jnp.concatenate(parts, 0)
        g_a[1 + i] += dot(g_t.astype(bf16), key_s[...])
        dkv_s[i] = jnp.transpose(g_t[:, M:]).astype(bf16)
    for dst, core in ((dkv_own, c), (dkv_oth, 1 - c)):
        for k in range(n_t):
            rows = pl.ds(pl.multiple_of(core * RQ + (t_me ^ k) * rr, rr), rr)
            dst[k] = jnp.concatenate([dkv_s[0, rows, :hc], dkv_s[1, rows, :hc]], 1)

    @pl.when(step == pl.num_programs(0) - 1)
    def _():
        gr = dot(gr_a[...].astype(bf16), table[...])
        for i in range(2):
            rows = slice(i * hc, (i + 1) * hc)
            last = g_a[2, :hc] if i == 0 else gr[:hc]
            first = g_a[i, :hc]
            gw_own[rows, :] = jnp.where(c == 0, first, last).astype(bf16)
            gw_oth[rows, :] = jnp.where(c == 0, last, first).astype(bf16)
        hi = sm_a[...].astype(bf16)
        lo = (sm_a[...] - hi.astype(f32)).astype(bf16)
        sums = jnp.concatenate([hi, lo], 0)
        for dst in (gw_own, gw_oth):
            dst[2 * hc :, : 2 * LANES] = sums
            dst[2 * hc :, 2 * LANES :] = jnp.zeros((SUM_ROWS, D - 2 * LANES), bf16)


def attn_bwd(meta, p, datt, kx, v, hid, qry, mem, hid_o, mem_o, segs, wq, rk, table, bw, br, bs, se):
    _, rh, _ = hid.shape
    count = p.shape[0]
    rm = mem.shape[1]
    hc = wq.shape[0]
    n_t = len(datt)
    rr = rh // n_t
    sds = jax.ShapeDtypeStruct
    g_shape = (2 * hc + SUM_ROWS, D)
    lanes = by_lane((rr, 2 * hc))
    both = pl.BlockSpec((n_t, rr, 2 * hc), lambda s, *_: (0, 0, s))
    grid_spec = pltpu.PrefetchScalarGridSpec(
        num_scalar_prefetch=1,
        grid=(count,),
        in_specs=[
            per_seq((1, 3, 2, rh, KT)), per_seq((1, KT, 3 * LANES)), per_seq((1, KT, 2 * LANES)),
            from_seq((1, rh, D)), from_seq((1, rh, D)), from_seq((1, rm, D)), from_seq((1, rh, D)), from_seq((1, rm, D)),
            whole(segs.shape), whole(wq.shape), whole(rk.shape), whole(table.shape),
            whole(bw.shape), whole(br.shape), whole(bs.shape), whole(se.shape),
        ] + [lanes] * n_t,
        out_specs=[lanes] * n_t + [both, both, whole(g_shape), whole(g_shape)],
        scratch_shapes=[
            pltpu.VMEM((2 * LANES, D), bf16), pltpu.VMEM((KT, D), bf16), pltpu.VMEM((2, RQ, 2 * LANES), bf16),
            pltpu.VMEM((2, RQ, D), bf16), pltpu.VMEM((2, RQ, 2 * LANES), bf16), pltpu.VMEM((2, RQ, 2 * LANES), bf16),
            pltpu.VMEM((2, RQ, 2 * LANES), f32), pltpu.VMEM((2, RQ, KT), bf16), pltpu.VMEM((2, 2, HB, WB), bf16),
            pltpu.VMEM((2, L, 2 * LANES), bf16), pltpu.VMEM((2, RQ, 2 * LANES), f32), pltpu.VMEM((2, RQ, 2 * LANES), f32),
            pltpu.VMEM((2, RQ, 2 * LANES), f32),
            pltpu.VMEM((3, 2 * LANES, D), f32), pltpu.VMEM((2 * LANES, WIN), f32), pltpu.VMEM((8, 2 * LANES), f32),
        ],
    )
    out = pl.pallas_call(
        attn_bwd_kernel,
        grid_spec=grid_spec,
        out_shape=[sds((rr, count * 2 * hc), bf16)] * n_t + [sds((n_t, rr, count * 2 * hc), bf16)] * 2
        + [sds(g_shape, bf16)] * 2,
        compiler_params=pltpu.CompilerParams(vmem_limit_bytes=58 << 20),
        cost_estimate=pl.CostEstimate(flops=count * 10**10, bytes_accessed=count * 16 * 10**6, transcendentals=0),
        name="attn_bwd",
    )(meta, p, kx, v, hid, qry, mem, hid_o, mem_o, segs, wq, rk, table, bw, br, bs, se, *datt)
    return out[:n_t], out[n_t], out[n_t + 1], out[n_t + 2 :]


def norm_bwd(d_out, scaled, inv_std, gain):
    e = d_out * gain
    return inv_std * (e - jnp.mean(e, -1, keepdims=True) - scaled * jnp.mean(e * scaled, -1, keepdims=True))


def norm_fwd(resid):
    cen = resid - jnp.mean(resid, -1, keepdims=True)
    inv_std = lax.rsqrt(jnp.mean(cen * cen, -1, keepdims=True) + EPS)
    return cen * inv_std, inv_std


GELU_A = 0.7978845608028654
GELU_B = 0.044715


def ffn_kernel(ti, *refs):
    n_t = (len(refs) - 47) // 4
    it = iter(refs)
    take = lambda n: [next(it) for _ in range(n)]
    att = [take(n_t) for _ in range(2)]
    (hid, qry, cot_h, cot_q, wi_own, wo_own, wx_own, wgot, n1g, n1b, bo, n2g, n2b) = take(13)
    datt_out = [take(n_t) for _ in range(2)]
    big_out = take(9)
    vec_out, gb_out = take(2)
    (wi, wo, wx, n1_s, sc1_s, inv1_s, gp_s, acc_s, dres2_s, x_s) = take(10)
    big = take(9)
    (out_h, out_q, dres_out, inner_out, act_out, dpre_out, dout_out, dattn_out, attr_out) = big
    sems, sems_x, sems_o, sems_k = take(4)
    t_me = ti[0]
    hc = attr_out.shape[2]
    rows = dres_out.shape[0]
    half = rows // 2
    n_p = wgot.shape[0]
    parts = ((wx, wx_own), (wi, wi_own), (wo, wo_own))

    def piece_copy(i, k, j):
        dst = parts[i][0]
        count = dst.shape[1] // n_p
        start = ((wi.shape[1] + wo.shape[1]) // n_p, 0, wi.shape[1] // n_p)[i]
        return pltpu.make_async_copy(
            wgot.at[j, k - 1, pl.ds(start, count), :], dst.at[k, pl.ds(j * count, count), :], sems.at[i, k, j]
        )

    copies = []
    for i, (dst, own) in enumerate(parts):
        group = [[pltpu.make_async_copy(own, dst.at[0], sems.at[i, 0, 0])]]
        group += [[piece_copy(i, k, j) for j in range(n_p)] for k in range(1, n_t)]
        copies.append(group)
    rr = x_s.shape[2]
    mine = [
        pltpu.make_async_copy(x.at[:, pl.ds(t_me * rr, rr), :], x_s.at[i], sems_x.at[i])
        for i, x in enumerate((hid, qry, cot_h, cot_q))
    ]
    for copy in mine[:2]:
        copy.start()
    for per_k in copies[0]:
        for copy in per_k:
            copy.start()
    for k in range(n_t):
        for copy in copies[1][k] + copies[2][k]:
            copy.start()
    for copy in mine[2:]:
        copy.start()
    leave = [pltpu.make_async_copy(big[i], big_out[i], sems_o.at[i]) for i in range(9)]
    leave_k = lambda i, k: pltpu.make_async_copy(big[4 + i].at[k], big_out[4 + i].at[k], sems_k.at[i, k])

    halves = (slice(0, half), slice(half, rows))
    for per_k in copies[0]:
        for copy in per_k:
            copy.wait()
    n_h = half // (2 * rr)
    for a in range(2):
        r = halves[a]
        mine[a].wait()
        acc = x_s[a].reshape(half, D).astype(f32)
        for k in range(n_t):
            pieces = [
                att[i][k][:, (2 * s + a) * hc : (2 * s + a + 1) * hc] for i in range(2) for s in range(n_h)
            ]
            part = jnp.concatenate(pieces, 0)
            attr_out[k, r, :] = part
            acc = acc + dot(part, wx[k, :hc, :])
        scaled, inv_std = norm_fwd(acc)
        sc1_s[r, :] = scaled
        inv1_s[r, :] = jnp.broadcast_to(inv_std, (half, LANES))
        n1 = scaled * n1g[...] + n1b[...]
        n1_s[r, :] = n1
        inner_out[r, :] = n1.astype(bf16)
    leave[8].start()
    leave[3].start()
    acc_s[...] = jnp.zeros(acc_s.shape, f32)

    def up(k, carry):
        @pl.when(k == 0)
        def _():
            copies[1][0][0].wait()
            copies[2][0][0].wait()

        @pl.when(k > 0)
        def _():
            for i in (1, 2):
                for j in range(n_p):
                    piece_copy(i, k, j).wait()

        bias = wx[k, hc : hc + 1, :].astype(f32) + wx[k, hc + 1 : hc + 2, :].astype(f32)
        for r in halves:
            pre = dot(inner_out[r, :], wi[k]) + bias
            sq = pre * pre
            th = jnp.tanh(GELU_A * (pre + GELU_B * (pre * sq)))
            act_out[k, r, :] = (0.5 * pre * (1.0 + th)).astype(bf16)
            gp_s[k, r, :] = 0.5 * (1.0 + th) + (0.5 * pre) * (1.0 - th * th) * (GELU_A + (3.0 * GELU_A * GELU_B) * sq)
            acc_s[r, :] += dot(act_out[k, r, :], wo[k])
        leave_k(0, k).start()
        return carry

    lax.fori_loop(0, n_t, up, 0)

    sums = [None] * 3
    for a, o_ref in enumerate((out_h, out_q)):
        r = halves[a]
        scaled, inv_std = norm_fwd(n1_s[r, :] + (acc_s[r, :] + bo[...]))
        o_ref[...] = scaled * n2g[...] + n2b[...]
        leave[a].start()
        mine[2 + a].wait()
        cot = x_s[2 + a].reshape(half, D).astype(f32)
        d2 = norm_bwd(cot, scaled, inv_std, n2g[...])
        dres2_s[r, :] = d2
        dout_out[r, :] = d2.astype(bf16)
        for i, g in enumerate((cot * scaled, cot, d2)):
            g = jnp.sum(g, 0, keepdims=True)
            sums[i] = g if a == 0 else sums[i] + g
    leave[6].start()
    vec_out[2:3, :] = sums[0]
    vec_out[3:4, :] = sums[1]
    vec_out[4:5, :] = sums[2]
    acc_s[...] = jnp.zeros(acc_s.shape, f32)

    def down(k, carry):
        total = None
        for r in halves:
            d_pre = dot_nt(dout_out[r, :], wo[k]) * gp_s[k, r, :]
            g = jnp.sum(d_pre, 0, keepdims=True)
            total = g if total is None else total + g
            dpre_out[k, r, :] = d_pre.astype(bf16)
            acc_s[r, :] += dot_nt(dpre_out[k, r, :], wi[k])
        gb_out[pl.ds(k, 1), :] = total
        leave_k(1, k).start()
        return carry

    lax.fori_loop(0, n_t, down, 0)
    for a in range(2):
        r = halves[a]
        d_n1 = dres2_s[r, :] + acc_s[r, :]
        scaled = sc1_s[r, :]
        for i, g in enumerate((d_n1 * scaled, d_n1)):
            g = jnp.sum(g, 0, keepdims=True)
            vec_out[i : i + 1, :] = g if a == 0 else vec_out[i : i + 1, :] + g
        d1 = norm_bwd(d_n1, scaled, inv1_s[r, :1], n1g[...])
        dres_out[r, :] = d1
        dattn_out[r, :] = d1.astype(bf16)
    leave[2].start()
    leave[7].start()
    for k in range(n_t):
        part = dot_nt(dattn_out[...], wx[k, :hc, :]).astype(bf16)
        for i in range(2):
            for s in range(n_h):
                first = (i * n_h + s) * rr
                datt_out[i][k][:, 2 * s * hc : (2 * s + 2) * hc] = jnp.concatenate(
                    [part[first : first + rr], part[half + first : half + first + rr]], 1
                )
    for i in (0, 1, 2, 3, 6, 7, 8):
        leave[i].wait()
    for i in range(2):
        for k in range(n_t):
            leave_k(i, k).wait()


def ffn(ti, att0, att1, hid, qry, cot_h, cot_q, w_inner, w_outer, wx_own, wgot, n1g, n1b, bo, n2g, n2b, hc):
    n_t = len(att0)
    n_f = w_outer.shape[0]
    n_s, rr = hid.shape[0], hid.shape[1] // n_t
    half = n_s * rr
    rows = 2 * half
    sds = jax.ShapeDtypeStruct
    hbm = pl.BlockSpec(memory_space=pl.ANY)
    big = [
        ((half, D), f32), ((half, D), f32), ((rows, D), f32), ((rows, D), bf16), ((n_t, rows, n_f), bf16),
        ((n_t, rows, n_f), bf16), ((rows, D), bf16), ((rows, D), bf16), ((n_t, rows, hc), bf16),
    ]
    out = pl.pallas_call(
        ffn_kernel,
        grid=(1,),
        in_specs=[pl.BlockSpec(memory_space=pltpu.SMEM)] + [whole(att0[0].shape)] * (2 * n_t) + [hbm] * 8
        + [whole((1, D))] * 5,
        out_specs=[whole(att0[0].shape)] * (2 * n_t) + [hbm] * len(big) + [whole((5, D)), whole((n_t, n_f))],
        out_shape=[sds(att0[0].shape, bf16)] * (2 * n_t) + [sds(*b) for b in big] + [sds((5, D), f32), sds((n_t, n_f), f32)],
        scratch_shapes=[
            pltpu.VMEM((n_t,) + w_inner.shape, bf16), pltpu.VMEM((n_t,) + w_outer.shape, bf16),
            pltpu.VMEM((n_t,) + wx_own.shape, bf16),
            pltpu.VMEM((rows, D), f32), pltpu.VMEM((rows, D), f32), pltpu.VMEM((rows, LANES), f32),
            pltpu.VMEM((n_t, rows, n_f), f32), pltpu.VMEM((rows, D), f32), pltpu.VMEM((rows, D), f32),
            pltpu.VMEM((4, n_s, rr, D), bf16),
        ] + [pltpu.VMEM(*b) for b in big] + [
            pltpu.SemaphoreType.DMA((3, n_t, wgot.shape[0])), pltpu.SemaphoreType.DMA((4,)),
            pltpu.SemaphoreType.DMA((len(big),)), pltpu.SemaphoreType.DMA((2, n_t)),
        ],
        compiler_params=pltpu.CompilerParams(vmem_limit_bytes=60 << 20),
        cost_estimate=pl.CostEstimate(flops=20 * 10**9, bytes_accessed=25 * 10**6, transcendentals=2 * 10**6),
        name="ffn",
    )(ti, *att0, *att1, hid, qry, cot_h, cot_q, w_inner, w_outer, wx_own, wgot, n1g, n1b, bo, n2g, n2b)
    return out[:n_t], out[n_t : 2 * n_t], out[2 * n_t : 2 * n_t + 9], out[2 * n_t + 9 :]


XROWS = 256


def wgrad_kernel(pos, inner, act, dpre, dout, attr, dattn, vec, gb, ga_out, own_out, oth_out, gx_s):
    hc = attr.shape[2]
    n_p = ga_out.shape[0]
    d, c = pos[0], pos[1]
    k = pl.program_id(0)
    z = pos[2] ^ k
    n_i, n_o, n_x = D // n_p, act.shape[2] // n_p, XROWS // n_p
    gx_s[:hc, :] = dot_tn(attr[0], dattn[...])
    gx_s[hc:, :] = jnp.zeros((gx_s.shape[0] - hc, D), f32)
    gx_s[hc : hc + 1, :] = gb[pl.ds(k, 1), :]
    for t in range(D // hc):
        @pl.when(z == t)
        def _():
            gx_s[hc + 8 : hc + 13, :hc] = vec[:, t * hc : (t + 1) * hc]
    n_a = ga_out.shape[2] - n_i
    g = dot_tn(inner[...], dpre[0]).astype(bf16)
    for j in range(n_p):
        ga_out[j, 0, :n_i] = g[j * n_i : (j + 1) * n_i]
    g = dot_tn(act[0], dout[...])
    for j in range(n_p):
        ga_out[j, 0, n_i:] = g[j * n_o : j * n_o + n_a].astype(bf16)
    for m in range(n_p // 2):
        halves = [
            jnp.concatenate([g[j * n_o + n_a : (j + 1) * n_o], gx_s[j * n_x : (j + 1) * n_x]], 0)
            for j in (2 * m, 2 * m + 1)
        ]
        own_out[m ^ d, 0] = jnp.where(c == 0, halves[0], halves[1]).astype(bf16)
        oth_out[m ^ d, 0] = jnp.where(c == 0, halves[1], halves[0]).astype(bf16)


def wgrad(pos, inner, act, dpre, dout, attr, dattn, vec, gb, n_d):
    n_t, rows, n_f = act.shape
    n_p = 2 * n_d
    n_o = n_f // n_p
    n_a = 2 * n_o // 3
    first = D // n_p + n_a
    rest = n_o - n_a + XROWS // n_p
    return pl.pallas_call(
        wgrad_kernel,
        grid=(n_t,),
        in_specs=[
            pl.BlockSpec(memory_space=pltpu.SMEM),
            whole(inner.shape), per_seq((1, rows, n_f)), per_seq((1, rows, n_f)), whole(dout.shape),
            per_seq((1,) + attr.shape[1:]), whole(dattn.shape), whole(vec.shape), whole(gb.shape),
        ],
        out_specs=[per_seq((n_p, 1, first, D), 1)] + [per_seq((n_d, 1, rest, D), 1)] * 2,
        out_shape=[
            jax.ShapeDtypeStruct((n_p, n_t, first, D), bf16)
        ] + [jax.ShapeDtypeStruct((n_d, n_t, rest, D), bf16)] * 2,
        scratch_shapes=[pltpu.VMEM((XROWS, D), f32)],
        compiler_params=pltpu.CompilerParams(vmem_limit_bytes=60 << 20),
        cost_estimate=pl.CostEstimate(flops=6 * 10**9, bytes_accessed=20 * 10**6, transcendentals=0),
        name="wgrad",
    )(pos, inner, act, dpre, dout, attr, dattn, vec, gb)


def final_kernel(*refs):
    n_t = (len(refs) - 10) // 2
    w_own, wgot, dres, gh, gq, w_s, rows_s, sems, sems_r, sems_d = refs[2 * n_t :]
    n_p = wgot.shape[0]
    half = gh.shape[0]
    rr = rows_s.shape[1] // 2
    n_h = half // (2 * rr)
    hc = rows_s.shape[2] // (2 * n_h)
    count = wgot.shape[2]
    copies = [[pltpu.make_async_copy(w_own, w_s.at[0], sems.at[0, 0])]]
    for k in range(1, n_t):
        copies.append([
            pltpu.make_async_copy(wgot.at[j, k - 1], w_s.at[k, pl.ds(j * count, count), :], sems.at[k, j])
            for j in range(n_p)
        ])
    row_copies = [pltpu.make_async_copy(refs[i], rows_s.at[i], sems_r.at[i]) for i in range(2 * n_t)]
    base = [pltpu.make_async_copy(dres.at[pl.ds(i * half, half), :], g, sems_d.at[i]) for i, g in enumerate((gh, gq))]
    for copy in base:
        copy.start()
    for k in range(n_t):
        for copy in [row_copies[k], row_copies[n_t + k]] + copies[k]:
            copy.start()
    for copy in base:
        copy.wait()
    for k in range(n_t):
        for copy in [row_copies[k], row_copies[n_t + k]] + copies[k]:
            copy.wait()
        wq, wk, wv = (w_s[k, i * hc : (i + 1) * hc, :] for i in range(3))

        def kind(low, i):
            return jnp.concatenate([
                rows_s[side * n_t + k, low : low + rr, (2 * s + i) * hc : (2 * s + i + 1) * hc]
                for side in range(2) for s in range(n_h)
            ], 0)

        gh[...] += dot(kind(0, 0), wq) + dot(kind(rr, 0), wk) + dot(kind(rr, 1), wv)
        gq[...] += dot(kind(0, 1), wq)


def final_proj(rows0, rows1, w_own, wgot, dres):
    half = dres.shape[0] // 2
    n_t = len(rows0)
    hbm = pl.BlockSpec(memory_space=pl.ANY)
    return pl.pallas_call(
        final_kernel,
        grid=(1,),
        in_specs=[hbm] * (2 * n_t + 3),
        out_specs=[whole((half, D))] * 2,
        out_shape=[jax.ShapeDtypeStruct((half, D), f32)] * 2,
        scratch_shapes=[
            pltpu.VMEM((n_t,) + w_own.shape, bf16), pltpu.VMEM((2 * n_t,) + rows0[0].shape, bf16),
            pltpu.SemaphoreType.DMA((n_t, wgot.shape[0])), pltpu.SemaphoreType.DMA((2 * n_t,)), pltpu.SemaphoreType.DMA((2,)),
        ],
        compiler_params=pltpu.CompilerParams(vmem_limit_bytes=60 << 20),
        cost_estimate=pl.CostEstimate(flops=2 * 10**9, bytes_accessed=8 * 10**6, transcendentals=0),
        name="final_proj",
    )(*rows0, *rows1, w_own, wgot, dres)


def unpack_kernel(pos, *refs):
    n_p = len(refs) - 10
    n_d = n_p // 2
    gi, go, gw, gx, gi_s, go_s, gx_s, got, sems, sems_g = refs[n_p:]
    d, c = pos[0], pos[1]
    hc = gw.shape[0]
    n_i, n_o, n_x = gi_s.shape[0] // n_p, go_s.shape[0] // n_p, gx_s.shape[0] // n_p
    arrive = []
    for m in range(n_d):
        for side in range(2):
            to = 2 * (m ^ d) + (c if side == 0 else 1 - c)
            arrive.append(pltpu.make_async_copy(refs[side * n_d + m], got.at[to], sems_g.at[side, m]))
    for copy in arrive:
        copy.start()
    copies = []
    for n, copy in enumerate(arrive):
        copy.wait()
        m, side = n // 2, n % 2
        to = 2 * (m ^ d) + (c if side == 0 else 1 - c)
        piece = got[to].astype(f32)
        parts = ((gi_s, gi, n_i, 0), (go_s, go, n_o, n_i), (gx_s, None, n_x, n_i + n_o))
        for i, (src, dst, count, first) in enumerate(parts):
            rows = pl.ds(pl.multiple_of(to * count, count), count)
            src[rows, :] = piece[first : first + count]
            if dst is not None:
                copies.append(pltpu.make_async_copy(src.at[rows, :], dst.at[rows, :], sems.at[i, n]))
                copies[-1].start()
    copies.append(pltpu.make_async_copy(gx_s.at[:hc, :], gw, sems.at[2, 0]))
    copies[-1].start()
    gx[...] = gx_s[hc:, :]
    for copy in copies:
        copy.wait()


def unpack(pos, own, oth, n_f, hc):
    hbm = pl.BlockSpec(memory_space=pl.ANY)
    n_p = 2 * len(own)
    shapes = [(D, n_f), (n_f, D), (hc, D), (XROWS - hc, D)]
    return pl.pallas_call(
        unpack_kernel,
        grid=(1,),
        in_specs=[pl.BlockSpec(memory_space=pltpu.SMEM)] + [hbm] * n_p,
        out_specs=[hbm] * 3 + [pl.BlockSpec(memory_space=pltpu.VMEM)],
        out_shape=[jax.ShapeDtypeStruct(shape, f32) for shape in shapes],
        scratch_shapes=[
            pltpu.VMEM((D, n_f), f32), pltpu.VMEM((n_f, D), f32), pltpu.VMEM((XROWS, D), f32),
            pltpu.VMEM((n_p,) + own[0].shape, bf16), pltpu.SemaphoreType.DMA((3, n_p)),
            pltpu.SemaphoreType.DMA((2, n_p // 2)),
        ],
        compiler_params=pltpu.CompilerParams(vmem_limit_bytes=60 << 20),
        name="unpack",
    )(pos, *own, *oth)


def unpack_heads_kernel(pos, own0, own1, oth0, oth1, gq, gk, gv, gr, b_word, b_rel, b_seg, g_seg):
    c = pos[1]
    hc = gq.shape[0]
    for i, g in enumerate((gq, gk, gv, gr)):
        own, oth = ((own0, oth0), (own1, oth1))[i % 2]
        g[...] = jnp.where(c == i // 2, own[:hc, :].astype(f32), oth[:hc, :].astype(f32))
    sums = own1[hc:, :hc].astype(f32)
    sums = sums[:8] + sums[8:]
    for h in range(hc // DH):
        cols = slice(h * DH, (h + 1) * DH)
        for row, dst in enumerate((b_word, b_rel, b_seg)):
            dst[h : h + 1, :] = sums[row : row + 1, cols]
        g_seg[h] = sums[3:5, cols]


def unpack_heads(pos, own, oth, hc):
    sds = jax.ShapeDtypeStruct
    heads = hc // DH
    shapes = [(hc, D)] * 4 + [(heads, DH)] * 3 + [(heads, 2, DH)]
    return pl.pallas_call(
        unpack_heads_kernel,
        grid=(1,),
        in_specs=[pl.BlockSpec(memory_space=pltpu.SMEM)] + [whole(x.shape) for x in own + oth],
        out_specs=[whole(shape) for shape in shapes],
        out_shape=[sds(shape, f32) for shape in shapes],
        compiler_params=pltpu.CompilerParams(vmem_limit_bytes=48 << 20),
        name="unpack_heads",
    )(pos, *own, *oth)


def table_rows(start, count):
    step = 32
    freq = 1.0 / 10000.0 ** (jnp.arange(0, D, 2).astype(f32) / D)
    coarse = (M + L - start - step * jnp.arange(count // step)).astype(f32)[:, None] * freq[None]
    fine = jnp.arange(step).astype(f32)[:, None] * freq[None]
    sin_c, cos_c = jnp.sin(coarse)[:, None], jnp.cos(coarse)[:, None]
    sin_f, cos_f = jnp.sin(fine)[None], jnp.cos(fine)[None]
    sin_a = sin_c * cos_f - cos_c * sin_f
    cos_a = cos_c * cos_f + sin_c * sin_f
    return jnp.concatenate([sin_a, cos_a], -1).reshape(count, D).astype(bf16)


def body(
    hidden, query, memory, cot_hidden, cot_query, lengths, ranks, segments,
    w_query, w_key, w_value, w_rel, w_out, bias_word, bias_rel, bias_seg, seg_embed,
    norm1_gain, norm1_bias, w_inner, b_inner, w_outer, b_outer, norm2_gain, norm2_bias,
):
    n_s, rh, _ = hidden.shape
    n_t = lax.axis_size("tensor")
    n_c = lax.axis_size("ctx")
    heads = bias_word.shape[0]
    hc = heads * DH
    n_f = w_inner.shape[1]
    rr = rh // n_t
    ci = lax.axis_index("ctx")
    ti = lax.axis_index("tensor")
    swap = [(i, (i + 1) % n_c) for i in range(n_c)]

    hid_o = lax.ppermute(hidden, "ctx", swap)
    mem_o = lax.ppermute(memory, "ctx", swap)

    n_d = lax.axis_size("dp")
    tile = 16
    di = lax.axis_index("dp")
    n_p = n_d * n_c
    while (D // n_p) % tile or (XROWS // n_p) % tile:
        n_p //= 2
    groups = n_d * n_c // n_p
    piece = (di * n_c + ci) // groups

    def across(x, k):
        return lax.ppermute(x, "tensor", [(i, i ^ k) for i in range(n_t)])

    tie = lax.optimization_barrier

    def send(own):
        return [across(own, k) for k in range(1, n_t)]

    def spread(got):
        return lax.all_gather(jnp.stack(got), ("dp", "ctx"), axis=0, tiled=False)[::groups]

    def cut(x):
        count = x.shape[0] // n_p
        return lax.dynamic_slice_in_dim(x, piece * count, count, 0)

    b_hi = b_inner.astype(bf16)
    b_lo = (b_inner - b_hi.astype(f32)).astype(bf16)
    wx = jnp.concatenate([w_out, b_hi[None], b_lo[None], jnp.zeros((XROWS - hc - 2, n_f), bf16)], 0)
    got = send(jnp.concatenate([cut(w_inner), cut(w_outer), cut(wx)], 0))
    wq, wk, wv, wr = (jnp.swapaxes(w, 0, 1) for w in (w_query, w_key, w_value, w_rel))
    w_t = jnp.concatenate([wq, wk, wv, jnp.zeros((640 - 3 * hc, D), bf16)], 0)
    ti1 = ti[None].astype(jnp.int32)
    pos = jnp.stack([di, ci, ti]).astype(jnp.int32)
    got_t = send(cut(w_t))

    table = table_rows(L - ci * rh - rh, WIN)
    wr_p = jnp.concatenate([wr, jnp.zeros((2 * LANES - hc, D), bf16)], 0)
    rk = lax.dot_general(table, wr_p, (((1,), (1,)), ((), ())), preferred_element_type=f32).astype(bf16)
    row = lambda v: jnp.pad(v.reshape(-1, hc), ((0, 0), (0, 2 * LANES - hc)))
    bw, br, bs, se = row(bias_word), row(bias_rel), row(bias_seg), row(seg_embed)

    half_s = n_s // 2
    metas = [
        jnp.concatenate([ci[None].astype(jnp.int32), lengths, ti1, jnp.full((1,), i * half_s, jnp.int32)]) for i in range(2)
    ]

    def forward(meta):
        return attn_fwd(
            meta, hidden, query, memory, hid_o, mem_o, ranks, segments, wq, wk, wv, rk, bw, br, bs, se, n_t, half_s
        )

    def share(own):
        return [own[0]] + [across(own[k], k) for k in range(1, n_t)]

    def along_dp(x, m):
        return lax.ppermute(x, "dp", [(i, i ^ m) for i in range(n_d)])

    def add(*terms):
        total = terms[0].astype(f32)
        for term in terms[1:]:
            total = total + term.astype(f32)
        return total.astype(bf16)

    def tie_all(*groups):
        flat = tie(tuple(x for group in groups for x in group))
        out, first = [], 0
        for group in groups:
            out.append(list(flat[first : first + len(group)]))
            first += len(group)
        return out

    att0, kept0 = forward(metas[0])
    att0, got = tie_all(att0, got)
    wgot = spread(got)
    att0 = share(att0)
    meta, _ = tie((metas[1], got[0]))
    att1, kept1 = forward(meta)
    att1, att0, got_t = tie_all(att1, att0, got_t)
    att1 = share(att1)
    vec1 = lambda x: x[None]
    got_t[0], _ = tie((got_t[0], wgot[0, 0, :1]))
    wgot_t = spread(got_t)
    datt0, datt1, big, (vec, gb) = ffn(
        ti1, att0, att1, hidden, query, cot_hidden, cot_query, w_inner, w_outer, wx, wgot,
        vec1(norm1_gain), vec1(norm1_bias), vec1(b_outer), vec1(norm2_gain), vec1(norm2_bias), hc,
    )
    out_h, out_q, dres, inner, act, dpre, dout, dattn, attr = big
    datt0 = share(datt0)
    ga, gb_own, gb_oth = wgrad(pos, inner, act, dpre, dout, attr, dattn, vec, gb, n_d)
    datt0, datt1, (ga, gb_oth, wgot_t) = tie_all(datt0, datt1, [ga, gb_oth, wgot_t])
    datt1 = share(datt1)
    gb_got = lax.ppermute(gb_oth, "ctx", swap)
    meta, ga = tie((metas[0], ga))
    ga = lax.psum_scatter(ga, ("dp", "ctx"), scatter_dimension=0, tiled=True)[0]

    def backward(meta, kept, datt):
        p, kx, v = kept
        return attn_bwd(
            meta, p, datt, kx, v, hidden, query, memory, hid_o, mem_o, segments, wq, rk, table, bw, br, bs, se
        )

    def payload(dq, dkv_own, dkv_oth):
        got = lax.ppermute(dkv_oth, "ctx", swap)
        return [jnp.concatenate([dq[k], add(dkv_own[k], got[k])], 0) for k in range(n_t)]

    dq, dkv_own, dkv_oth, gw0 = backward(meta, kept0, datt0)
    (dkv_oth, gb_got), datt1 = tie_all([dkv_oth, gb_got], datt1)
    pay = payload(dq, dkv_own, dkv_oth)
    gb = [add(gb_own[m], gb_got[m]) for m in range(n_d)]
    (meta,), pay, gb = tie_all([metas[1]], pay, gb)
    rows0 = share(pay)
    gb_got = [along_dp(gb[m], m) for m in range(1, n_d)]
    dq, dkv_own, dkv_oth, gw1 = backward(meta, kept1, datt1)
    (dkv_oth, ga), rows0, gw1, gb_got = tie_all([dkv_oth, ga], rows0, gw1, gb_got)

    total = [jnp.concatenate([ga[k], add(gb[0][k], *[g[k] for g in gb_got])], 0) for k in range(n_t)]
    total_got = [across(total[k], k) for k in range(1, n_t)]
    pay = payload(dq, dkv_own, dkv_oth)
    got_w = lax.ppermute(add(gw0[1], gw1[1]), "ctx", swap)
    part = [add(gw0[0][:hc], gw1[0][:hc], got_w[:hc]), add(gw0[0][hc:], gw1[0][hc:], got_w[hc:])]
    masks = [1 << i for i in range(n_d.bit_length() - 1)]
    for m0, m1 in zip(masks, masks[::-1]):
        part_got = [along_dp(part[0], m0), along_dp(part[1], m1)]
        part = [add(part[0], part_got[0]), add(part[1], part_got[1])]
    part_o = [lax.ppermute(x, "ctx", swap) for x in part]
    part, part_o, pay, total_got = tie_all(part, part_o, pay, total_got)
    total = add(total[0], *total_got)

    pay, (total,) = tie_all(pay, [total])
    others = [along_dp(total, m) for m in range(1, n_d)]
    rows1 = share(pay)
    heads_out = unpack_heads(pos, part, part_o, hc)
    heads_out, others = tie_all(heads_out, others)
    gwt = [jnp.swapaxes(g, 0, 1) for g in heads_out[:4]]
    pieces = [total] + others
    pieces_o = [lax.ppermute(x, "ctx", swap) for x in pieces]
    grad_h, grad_q = final_proj(rows0, rows1, w_t, wgot_t, dres)
    g_inner, g_outer, g_wout, g_x = unpack(pos, pieces, pieces_o, n_f, hc)
    vecs = g_x[8:13, :hc]
    shape = (n_s, rr, D)
    return (
        out_h.reshape(shape), out_q.reshape(shape), grad_h.reshape(shape), grad_q.reshape(shape),
        gwt[0], gwt[1], gwt[2], gwt[3], g_wout,
        heads_out[4], heads_out[5], heads_out[6], jnp.swapaxes(heads_out[7], 0, 1),
        vecs[0], vecs[1], g_inner, g_x[0], g_outer,
        vecs[4], vecs[2], vecs[3],
    )


def solution(mesh):
    rows = P("dp", "ctx", None)
    by_col = P(None, "tensor")
    by_row = P("tensor", None)
    own_rows = P("dp", ("ctx", "tensor"), None)
    vec = P("tensor")
    return jax.shard_map(
        body,
        mesh=mesh,
        in_specs=(
            rows, rows, rows, rows, rows, P("dp"), P("dp", None), P("dp", None),
            by_col, by_col, by_col, by_col, by_row, by_row, by_row, by_row, P(None, "tensor", None),
            P(), P(), by_col, vec, by_row, P(), P(), P(),
        ),
        out_specs=(
            own_rows, own_rows, own_rows, own_rows,
            by_col, by_col, by_col, by_col, by_row, by_row, by_row, by_row, P(None, "tensor", None),
            vec, vec, by_col, vec, by_row, vec, vec, vec,
        ),
        check_vma=False,
    )
```
